32 devices in a mesh: grp: 2 (over y), lon: 4 (over z), ch: 2 (over core), lat: 2 (over x).
Axes of the slice: x: 2, y: 2, z: 4, core: 2. Of those that a mesh axis runs over, the one named last changes fastest.
Arguments:
- inputs: bfloat16 [64, 512, 256], P(('grp', 'lat'), 'lon', 'ch'), parts along dimension 0, may hold values from -6 to 6
- cotangent: bfloat16 [64, 512, 256], P(('grp', 'lat'), 'lon', 'ch'), parts along dimension 0, may hold values from -6 to 6
- kernels: bfloat16 [2, 49, 256], P(None, None, 'ch'), may hold values from -0.875 to 0.875
- gains: float32 [2, 256], replicated, may hold values from 0.1 to 1.9
- w_in: bfloat16 [2, 256, 1024], P(None, None, 'ch'), may hold values from -0.375 to 0.375
- w_out: bfloat16 [2, 1024, 256], P(None, 'ch'), may hold values from -0.1875 to 0.1875
Outputs:
- grad_input: bfloat16 [64, 512, 256], P(('grp', 'lat'), 'lon', 'ch'), parts along dimension 0
- grad_w1: float32 [4, 256, 1024], P('grp', None, 'ch'), parts along dimension 0
- grad_w2: float32 [4, 1024, 256], P('grp', 'ch'), parts along dimension 0
- grad_kernel: float32 [4, 49, 256], P('grp', None, 'ch'), parts along dimension 0
The draws below stay inside these ranges and needn't reach their ends.
There are 2 independent parts, one for each index of `grp`. The reference program is written for one: setup_inputs(seed, part) draws one part's arguments, and reference() takes and returns one part's arrays. A program takes and returns all parts, laid end to end along the dimension named above; an argument that names none is the same for every part. Nothing has to cross between parts.
All inputs are finite; a program needn't handle non-finite values.
Results may differ from the reference program's by a relative error of at most 0.008.
Values may be sent and summed in bfloat16 or wider, within the bound.
No kernel may reach another device: no remote copies, remote signals or barrier semaphores. Data moves between devices by JAX's collectives and lax.ppermute only.
A program may use at most 128 MiB of HBM per device.

```python
import math
import jax
import jax.numpy as jnp
from jax import lax

C = 256
HID = 1024
BLOCKS = 2
LAT = 32
LON = 512


def steps_of(own_key, shape, shards, least, largest):
    loudness, own = 1.0, jax.random.fold_in(own_key, 6)
    for position, shards_of in shards:
        steps = jnp.exp(jax.random.uniform(jax.random.fold_in(own, position), (shards_of,), jnp.float32, least / len(shards), largest / len(shards)))
        loudness = loudness * jnp.repeat(steps, shape[position] // shards_of).reshape([-1 if axis == position else 1 for axis in range(len(shape))])
    return loudness


def normal_values(own_key, shape, spread, most, cuts=(), held_as=jnp.bfloat16):
    result = jax.random.normal(own_key, shape, jnp.float32) * spread
    if len(cuts) > 0:
        result = steps_of(own_key, shape, cuts, -0.22, 0.18) * result
    return jnp.clip(result, min=-most, max=most).astype(held_as)


def setup_inputs(seed: int = 0, part: int = 0) -> dict:
    key_of = jax.random.split(jax.random.key(seed), 7)
    part_keys = jax.random.split(jax.random.fold_in(key_of[6], part), 7)
    return {
        "inputs": normal_values(part_keys[0], (LAT, LON, C), 1.0, 6.0, ((0, 2), (1, 4), (2, 2))),
        "cotangent": normal_values(part_keys[1], (LAT, LON, C), 1.0, 6.0, ((0, 2), (1, 4), (2, 2))),
        "kernels": normal_values(key_of[2], (BLOCKS, 49, C), 49 ** -0.5, 0.875, ((2, 2),)),
        "gains": jnp.clip(1.0 + 0.18 * jax.random.normal(key_of[3], (BLOCKS, C), jnp.float32), 0.1, 1.9),
        "w_in": normal_values(key_of[4], (BLOCKS, C, HID), C ** -0.5, 0.375, ((2, 2),)),
        "w_out": normal_values(key_of[5], (BLOCKS, HID, C), HID ** -0.5, 0.1875, ((1, 2),)),
    }


def widen(source):
    wrapped = jnp.concatenate([source[:, -12:], source, source[:, :12]], axis=1)
    return jnp.pad(wrapped, ((12, 12), (0, 0), (0, 0)))

def forward_taps(widened, kernel_set):
    height = widened.shape[0] - 24
    breadth = widened.shape[1] - 24
    running = jnp.zeros((height, breadth, widened.shape[2]), jnp.float32)
    for row_tap in range(7):
        for col_tap in range(7):
            weights = kernel_set[7 * row_tap + col_tap].astype(jnp.float32)
            window = widened[4 * row_tap:4 * row_tap + height, 4 * col_tap:4 * col_tap + breadth]
            running = running + weights * window.astype(jnp.float32)
    return running

def backward_taps(widened, kernel_set):
    height = widened.shape[0] - 24
    breadth = widened.shape[1] - 24
    running = jnp.zeros((height, breadth, widened.shape[2]), jnp.float32)
    for row_tap in range(7):
        for col_tap in range(7):
            weights = kernel_set[7 * row_tap + col_tap].astype(jnp.float32)
            window = widened[24 - 4 * row_tap:24 - 4 * row_tap + height, 24 - 4 * col_tap:24 - 4 * col_tap + breadth]
            running = running + weights * window.astype(jnp.float32)
    return running

def tap_grads(widened, grad_conv):
    height = grad_conv.shape[0]
    breadth = grad_conv.shape[1]
    upstream = grad_conv.astype(jnp.float32)
    results = []
    for row_tap in range(7):
        for col_tap in range(7):
            window = widened[4 * row_tap:4 * row_tap + height, 4 * col_tap:4 * col_tap + breadth]
            results.append(lax.optimization_barrier(jnp.sum(window.astype(jnp.float32) * upstream, axis=(0, 1))))
    return jnp.stack(results)

def normalize(convolved, gain_row):
    centre = lax.optimization_barrier(jnp.mean(convolved, axis=-1, keepdims=True))
    centred = convolved - centre
    variance = lax.optimization_barrier(jnp.mean(centred * centred, axis=-1, keepdims=True))
    inverse_std = lax.rsqrt(variance + 1e-06)
    normalised = centred * inverse_std
    return ((normalised * gain_row).astype(jnp.bfloat16), normalised, inverse_std)

def reference(inputs, cotangent, kernels, gains, w_in, w_out):
    cell_count = LAT * LON
    current = inputs
    saved = []
    for layer_index in range(2):
        widened = widen(current)
        convolved = forward_taps(widened, kernels[layer_index]).astype(jnp.bfloat16)
        normed_in, normalised, inverse_std = normalize(convolved.astype(jnp.float32), gains[layer_index])
        flattened = normed_in.reshape(cell_count, C)
        preact = jnp.dot(flattened, w_in[layer_index], preferred_element_type=jnp.float32)
        hidden = jax.nn.gelu(preact).astype(jnp.bfloat16)
        saved.append((widened, flattened, normalised.reshape(cell_count, C), inverse_std.reshape(cell_count, 1), preact, hidden))
        if layer_index == 0:
            mixture = jnp.dot(hidden, w_out[0], preferred_element_type=jnp.float32)
            current = (current.astype(jnp.float32) + mixture.reshape(current.shape)).astype(jnp.bfloat16)
    adjoint_now = cotangent
    in_grads = [None, None]
    out_grads = [None, None]
    tap_list = [None, None]
    for layer_index in (1, 0):
        widened, flattened, normalised, inverse_std, preact, hidden = saved[layer_index]
        grad_flat = adjoint_now.reshape(cell_count, C)
        out_grads[layer_index] = jnp.dot(hidden.T, grad_flat, preferred_element_type=jnp.float32)
        into_hidden = jnp.dot(grad_flat, w_out[layer_index].T, preferred_element_type=jnp.float32)
        unused, pullback = jax.vjp(jax.nn.gelu, preact)
        pre_grad = pullback(into_hidden)[0].astype(jnp.bfloat16)
        in_grads[layer_index] = jnp.dot(flattened.T, pre_grad, preferred_element_type=jnp.float32)
        normed_grad = jnp.dot(pre_grad, w_in[layer_index].T, preferred_element_type=jnp.float32)
        weighted = normed_grad * gains[layer_index]
        centre_term = lax.optimization_barrier(jnp.mean(weighted, axis=-1, keepdims=True))
        slope_term = lax.optimization_barrier(jnp.mean(weighted * normalised, axis=-1, keepdims=True))
        grad_conv = ((weighted - centre_term - normalised * slope_term) * inverse_std).astype(jnp.bfloat16)
        grad_conv = grad_conv.reshape(adjoint_now.shape)
        tap_list[layer_index] = tap_grads(widened, grad_conv)
        spread_back = backward_taps(widen(grad_conv), kernels[layer_index])
        adjoint_now = (adjoint_now.astype(jnp.float32) + spread_back).astype(jnp.bfloat16)
    scaling = 1.0 / math.sqrt(cell_count)
    return (adjoint_now, jnp.stack(in_grads) * scaling, jnp.stack(out_grads) * scaling, jnp.stack(tap_list) * scaling)
```

```python
import math

import jax
import jax.numpy as jnp
from jax import lax
from jax.sharding import PartitionSpec as P

BF = jnp.bfloat16
F32 = jnp.float32


def halo_stage(block, axis, dim, periodic):
    count = lax.axis_size(axis)
    forward = [(i, i + 1) for i in range(count - 1)]
    if periodic:
        forward.append((count - 1, 0))
    backward = [(target, source) for source, target in forward]
    size = block.shape[dim]
    tail = lax.slice_in_dim(block, size - 12, None, axis=dim)
    head = lax.slice_in_dim(block, 0, 12, axis=dim)
    if count == 2 and not periodic:
        index = lax.axis_index(axis)
        got = lax.ppermute(jnp.where(index == 0, tail, head), axis, [(0, 1), (1, 0)])
        zero = jnp.zeros_like(got)
        low = jnp.where(index == 0, zero, got)
        high = jnp.where(index == 0, got, zero)
    else:
        low = lax.ppermute(tail, axis, forward)
        high = lax.ppermute(head, axis, backward)
    return jnp.concatenate([low, block, high], axis=dim)


def widen(source):
    return halo_stage(halo_stage(source, "lon", 1, True), "lat", 0, False)


def conv(widened, kernel_set, transposed):
    height = widened.shape[0] - 24
    breadth = widened.shape[1] - 24
    running = jnp.zeros((height, breadth, widened.shape[2]), F32)
    for row_tap in range(7):
        for col_tap in range(7):
            weights = kernel_set[7 * row_tap + col_tap].astype(F32)
            r, c = (6 - row_tap, 6 - col_tap) if transposed else (row_tap, col_tap)
            window = widened[4 * r : 4 * r + height, 4 * c : 4 * c + breadth]
            running = running + weights * window.astype(F32)
    return running


def tap_grads(widened, grad_conv):
    height, breadth = grad_conv.shape[:2]
    upstream = grad_conv.astype(F32)
    results = []
    for row_tap in range(7):
        for col_tap in range(7):
            window = widened[
                4 * row_tap : 4 * row_tap + height, 4 * col_tap : 4 * col_tap + breadth
            ]
            results.append(jnp.sum(window.astype(F32) * upstream, axis=(0, 1)))
    return jnp.stack(results)


def swap(x):
    return lax.ppermute(x, "ch", [(0, 1), (1, 0)])


def rows_of(x, which):
    half = x.shape[0] // 2
    return lax.dynamic_slice_in_dim(x, which * half, half, 0)


def to_cells(field):
    me = lax.axis_index("ch")
    theirs = swap(rows_of(field, 1 - me))
    mine = rows_of(field, me)
    both = jnp.concatenate([mine, theirs], axis=-1)
    return both.reshape(-1, both.shape[-1])


def to_field(cells, rows):
    me = lax.axis_index("ch")
    own = cells.shape[1] // 2
    theirs = swap(cells[:, own:])
    mine = cells[:, :own]
    pair = jnp.where(me == 0, jnp.concatenate([mine, theirs]), jnp.concatenate([theirs, mine]))
    return pair.reshape(rows, -1, own)


def normalize(convolved, gain_row):
    centre = jnp.mean(convolved, axis=-1, keepdims=True)
    centred = convolved - centre
    variance = jnp.mean(centred * centred, axis=-1, keepdims=True)
    inverse_std = lax.rsqrt(variance + 1e-06)
    normalised = centred * inverse_std
    return ((normalised * gain_row).astype(BF), normalised, inverse_std)


def norm_back(grad, normalised, inverse_std, gain_row):
    weighted = grad * gain_row
    centre_term = jnp.mean(weighted, axis=-1, keepdims=True)
    slope_term = jnp.mean(weighted * normalised, axis=-1, keepdims=True)
    return ((weighted - centre_term - normalised * slope_term) * inverse_std).astype(BF)


def dot(a, b, contract):
    return lax.dot_general(a, b, ((contract[0:1], contract[1:2]), ((), ())), preferred_element_type=F32)


def halving(axes):
    lon = lax.axis_size("lon")
    lat = lax.axis_size("lat")
    steps = []
    dist = 1
    while dist < lon:
        steps.append(("lon", dist))
        dist *= 2
    extra = []
    dist = 1
    while dist < lat:
        extra.append(("lat", dist))
        dist *= 2
    return steps[:1] + extra + steps[1:]


def grid_sum(part):
    steps = halving(None)

    def partner(x, axis, dist):
        count = lax.axis_size(axis)
        return lax.ppermute(x, axis, [(i, i ^ dist) for i in range(count)])

    for axis, dist in steps:
        bit = (lax.axis_index(axis) // dist) % 2
        half = part.shape[0] // 2
        keep = lax.dynamic_slice_in_dim(part, bit * half, half, 0)
        send = lax.dynamic_slice_in_dim(part, (1 - bit) * half, half, 0)
        part = keep + partner(send.astype(BF), axis, dist).astype(F32)
    part = part.astype(BF)
    for axis, dist in reversed(steps):
        bit = (lax.axis_index(axis) // dist) % 2
        got = partner(part, axis, dist)
        part = jnp.where(bit == 0, jnp.concatenate([part, got]), jnp.concatenate([got, part]))
    return part


def pick(me, own, other, axis):
    return jnp.where(
        me == 0, jnp.concatenate([own, other], axis), jnp.concatenate([other, own], axis)
    )


def on_device(inputs, cotangent, kernels, gains, w_in, w_out):
    rows = inputs.shape[0]
    own = inputs.shape[2]
    lat_total = rows * lax.axis_size("lat")
    lon_total = inputs.shape[1] * lax.axis_size("lon")
    scaling = 1.0 / math.sqrt(lat_total * lon_total)
    me = lax.axis_index("ch")

    def own_first(x, axis):
        half = x.shape[axis] // 2
        first = lax.dynamic_slice_in_dim(x, me * half, half, axis)
        second = lax.dynamic_slice_in_dim(x, (1 - me) * half, half, axis)
        return jnp.concatenate([first, second], axis)

    w_in_full = own_first(jnp.concatenate([w_in, swap(w_in)], axis=2), 1)
    w_out_full = own_first(jnp.concatenate([w_out, swap(w_out)], axis=1), 2)
    gains_full = own_first(gains, 1)

    widened0 = widen(inputs)
    conv0 = to_cells(conv(widened0, kernels[0], False).astype(BF))
    grad2 = to_cells(cotangent)
    y0, _, _ = normalize(conv0.astype(F32), gains_full[0])
    hid0 = jax.nn.gelu(dot(y0, w_in_full[0], (1, 0))).astype(BF)
    mix0 = dot(hid0, w_out_full[0], (1, 0)).astype(BF)
    current = (inputs.astype(F32) + to_field(mix0, rows).astype(F32)).astype(BF)
    widened1 = widen(current)
    conv1 = to_cells(conv(widened1, kernels[1], False).astype(BF))

    def back(b, conv_cells, grad):
        y, normalised, inverse_std = normalize(conv_cells.astype(F32), gains_full[b])
        pre = dot(y, w_in_full[b], (1, 0))
        hid, pullback = jax.vjp(jax.nn.gelu, pre)
        dwo = dot(hid.astype(BF), grad, (0, 0))
        dpre = pullback(dot(grad, w_out_full[b], (1, 1)))[0].astype(BF)
        dwi = dot(y, dpre, (0, 0))
        dy = dot(dpre, w_in_full[b], (1, 1))
        dconv = norm_back(dy, normalised, inverse_std, gains_full[b])
        return to_field(dconv, rows), dwi, dwo

    def weight_sums(dwi, dwo):
        half = dwi.shape[1] // 2
        got_i = swap(dwi[:, half:].astype(BF)).astype(F32)
        got_o = swap(dwo[half:].astype(BF)).astype(F32)
        wi = pick(me, dwi[:own, :half] + got_i[own:], dwi[own:, :half] + got_i[:own], 0)
        wo = pick(me, dwo[:half, :own] + got_o[:, own:], dwo[:half, own:] + got_o[:, :own], 1)
        cols = wo.shape[1]
        summed = grid_sum(jnp.concatenate([wi.reshape(-1, cols), wo])).astype(F32) * scaling
        return summed[: wi.size // cols].reshape(wi.shape), summed[wi.size // cols :]

    def tap_sum(dk):
        padded = jnp.pad(dk, ((0, 64 - dk.shape[0]), (0, 0)))
        return grid_sum(padded).astype(F32)[: dk.shape[0]] * scaling

    dconv1, dwi1, dwo1 = back(1, conv1, grad2)
    gwi1, gwo1 = weight_sums(dwi1, dwo1)
    gk1 = tap_sum(tap_grads(widened1, dconv1))
    grad1 = (cotangent.astype(F32) + conv(widen(dconv1), kernels[1], True)).astype(BF)
    dconv0, dwi0, dwo0 = back(0, conv0, to_cells(grad1))
    gwi0, gwo0 = weight_sums(dwi0, dwo0)
    gk0 = tap_sum(tap_grads(widened0, dconv0))
    grad0 = (grad1.astype(F32) + conv(widen(dconv0), kernels[0], True)).astype(BF)
    return (grad0, jnp.stack([gwi0, gwi1]), jnp.stack([gwo0, gwo1]), jnp.stack([gk0, gk1]))


def solution(mesh):
    return jax.shard_map(
        on_device,
        mesh=mesh,
        in_specs=(
            P(("grp", "lat"), "lon", "ch"),
            P(("grp", "lat"), "lon", "ch"),
            P(None, None, "ch"),
            P(),
            P(None, None, "ch"),
            P(None, "ch", None),
        ),
        out_specs=(
            P(("grp", "lat"), "lon", "ch"),
            P("grp", None, "ch"),
            P("grp", "ch", None),
            P("grp", None, "ch"),
        ),
        check_vma=False,
    )
```

```python
import math

import jax
import jax.numpy as jnp
from jax import lax
from jax.experimental import pallas as pl
from jax.experimental.pallas import tpu as pltpu
from jax.sharding import PartitionSpec as P

BF = jnp.bfloat16
F32 = jnp.float32


TILE = 32


def call(kernel, **kwargs):
    return pl.pallas_call(
        kernel,
        compiler_params=pltpu.CompilerParams(vmem_limit_bytes=48 * 2**20),
        **kwargs,
    )


VM = pl.BlockSpec(memory_space=pltpu.VMEM)
SM = pl.BlockSpec(memory_space=pltpu.SMEM)


def spread(wide, shifted, rows, pieces):
    for first, value in pieces:
        wide[:, first : first + value.shape[1], :] = value[...].astype(F32)
    shifted[...] = wide[:, 4 : 4 + shifted.shape[1], :]


def window(wide, shifted, row, tile, col_tap, cols):
    if col_tap % 2:
        return wide[row, pl.ds(pl.multiple_of(tile * cols + 4 * col_tap + 4, 8), cols), :]
    return shifted[row, pl.ds(pl.multiple_of(tile * cols + 4 * col_tap, 8), cols), :]


def wide_shapes(rows, breadth):
    return [pltpu.VMEM((rows, breadth + 32, 128), F32), pltpu.VMEM((rows, breadth + 24, 128), F32)]


def conv_local(block, low, high, weights):
    rows, breadth, chans = block.shape
    groups = rows // 4

    def kernel(block_ref, low_ref, high_ref, w_ref, out_ref, wide, shifted):
        spread(wide, shifted, rows, ((16, block_ref), (4, low_ref), (16 + breadth, high_ref)))
        tiles = breadth // TILE

        def step(i, carry):
            cls, tile = i // tiles, i % tiles
            sums = [jnp.zeros((TILE // 8, 8, chans), F32) for _ in range(groups)]
            for q in range(7):
                taps = {}
                for r in range(groups):
                    v = window(wide, shifted, 4 * r + cls, tile, q, TILE).reshape(-1, 8, chans)
                    for k in range(groups):
                        p = r - k + 3
                        if 0 <= p <= 6:
                            if p not in taps:
                                taps[p] = w_ref[7 * p + q : 7 * p + q + 1, :]
                            sums[k] = sums[k] + taps[p] * v
            for k in range(groups):
                out_ref[4 * k + cls, pl.ds(pl.multiple_of(tile * TILE, 8), TILE), :] = sums[
                    k
                ].reshape(TILE, chans)
            return carry

        lax.fori_loop(0, 4 * tiles, step, 0)

    return call(
        kernel,
        in_specs=[VM] * 4,
        out_specs=VM,
        out_shape=jax.ShapeDtypeStruct(block.shape, F32),
        scratch_shapes=wide_shapes(rows, breadth),
        name="conv_local",
    )(block, low, high, weights)


def conv_remote(meta, sums_in, got, weights, base=None, last=True):
    rows, breadth, chans = sums_in.shape
    groups = rows // 4
    half = rows // 2

    def kernel(meta_ref, sums_ref, got_ref, w_ref, *rest):
        if base is not None:
            base_ref, rest = rest[0], rest[1:]
        if last:
            out_ref, send_ref, wide, shifted = rest
        else:
            out_ref, wide, shifted = rest
        below = meta_ref[0]
        spread(wide, shifted, 12, ((4, got_ref),))
        tiles = breadth // TILE

        def mirror(x, most):
            return x + below * (most - 2 * x)

        def step(i, carry):
            cls, tile = i // tiles, i % tiles
            cols = pl.ds(pl.multiple_of(tile * TILE, 8), TILE)
            at = [4 * mirror(k, groups - 1) + cls for k in range(groups)]
            sums = [sums_ref[at[k], cols, :].reshape(-1, 8, chans) for k in range(groups)]
            for q in range(7):
                taps = [w_ref[pl.ds(7 * mirror(p, 6) + q, 1), :] for p in range(3)]
                for r in range(3):
                    v = window(wide, shifted, 4 * mirror(r, 2) + cls, tile, q, TILE)
                    v = v.reshape(-1, 8, chans)
                    for k in range(min(groups, r + 1)):
                        sums[k] = sums[k] + taps[r - k] * v
            for k in range(groups):
                value = sums[k].reshape(TILE, chans)
                if base is not None:
                    value = value + base_ref[at[k], cols, :].astype(F32)
                out_ref[at[k], cols, :] = value.astype(out_ref.dtype)
            return carry

        lax.fori_loop(0, 4 * tiles, step, 0)
        if last:
            send_ref[...] = out_ref[pl.ds((1 - meta_ref[1]) * half, half)]

    field = jax.ShapeDtypeStruct((rows, breadth, chans), BF if last else F32)
    part = jax.ShapeDtypeStruct((half, breadth, chans), BF)
    args = (meta, sums_in, got, weights) + (() if base is None else (base,))
    return call(
        kernel,
        in_specs=[SM] + [VM] * (len(args) - 1),
        out_specs=(VM, VM) if last else VM,
        out_shape=(field, part) if last else field,
        scratch_shapes=wide_shapes(12, breadth),
        name="conv_remote",
    )(*args)


def tap_sums(meta, grad, block, low, high, gots):
    rows, breadth, chans = block.shape
    groups = rows // 4
    count = len(gots)

    def kernel(meta_ref, grad_ref, block_ref, low_ref, high_ref, *rest):
        got_refs, (out_ref, g_ref, wide, shifted, rwide, rshifted) = rest[:count], rest[count:]
        g_ref[...] = grad_ref[...].astype(F32)
        spread(wide, shifted, rows, ((16, block_ref), (4, low_ref), (16 + breadth, high_ref)))
        tiles = breadth // 8

        def near(cols_taps):
            def step(i, sums):
                cls, tile = i // tiles, i % tiles
                sums = list(sums)
                cols = pl.ds(pl.multiple_of(tile * 8, 8), 8)
                g = [g_ref[4 * k + cls, cols, :] for k in range(groups)]
                for n, q in enumerate(cols_taps):
                    for r in range(groups):
                        v = window(wide, shifted, 4 * r + cls, tile, q, 8)
                        for k in range(groups):
                            p = r - k + 3
                            if 0 <= p <= 6:
                                sums[7 * n + p] = sums[7 * n + p] + g[k] * v
                return tuple(sums)

            zero = jnp.zeros((8, chans), F32)
            sums = lax.fori_loop(0, 4 * tiles, step, (zero,) * (7 * len(cols_taps)))
            for n, q in enumerate(cols_taps):
                for p in range(7):
                    out_ref[7 * p + q : 7 * p + q + 1, :] = jnp.sum(
                        sums[7 * n + p], axis=0, keepdims=True
                    )

        def far(index, cols_taps):
            below = meta_ref[index]

            def mirror(x, most):
                return x + below * (most - 2 * x)

            def step(i, sums):
                cls, tile = i // tiles, i % tiles
                sums = list(sums)
                cols = pl.ds(pl.multiple_of(tile * 8, 8), 8)
                near_k = range(min(3, groups))
                g = [g_ref[4 * mirror(k, groups - 1) + cls, cols, :] for k in near_k]
                for n, q in enumerate(cols_taps):
                    for r in range(3):
                        v = window(rwide, rshifted, 4 * mirror(r, 2) + cls, tile, q, 8)
                        for k in near_k:
                            if k <= r:
                                sums[3 * n + r - k] = sums[3 * n + r - k] + g[k] * v
                return tuple(sums)

            zero = jnp.zeros((8, chans), F32)
            sums = lax.fori_loop(0, 4 * tiles, step, (zero,) * (3 * len(cols_taps)))
            for n, q in enumerate(cols_taps):
                for p in range(3):
                    at = pl.ds(7 * mirror(p, 6) + q, 1)
                    out_ref[at, :] = out_ref[at, :] + jnp.sum(
                        sums[3 * n + p], axis=0, keepdims=True
                    )

        for cols_taps in ((0, 2, 4, 6), (1, 3, 5)):
            near(cols_taps)
        for index in range(count):
            spread(rwide, rshifted, 12, ((4, got_refs[index]),))
            far(index, tuple(range(7)))

    return call(
        kernel,
        in_specs=[SM] + [VM] * (4 + count),
        out_specs=VM,
        out_shape=jax.ShapeDtypeStruct((49, chans), F32),
        scratch_shapes=[pltpu.VMEM(block.shape, F32)]
        + wide_shapes(rows, breadth)
        + wide_shapes(12, breadth),
        name="tap_sums",
    )(meta, grad, block, low, high, *gots)


CUBIC = 0.044715
ROOT = math.sqrt(2.0 / math.pi)


def layer_norm(x):
    centred = x - jnp.mean(x, axis=-1, keepdims=True)
    inverse = lax.rsqrt(jnp.mean(centred * centred, axis=-1, keepdims=True) + 1e-06)
    return centred * inverse, inverse


def mxu(a, b):
    return jnp.dot(a, b, preferred_element_type=F32)


STEP = 256


def cell_specs(cells, chans):
    steps = cells // STEP
    mine = pl.BlockSpec((STEP, chans), lambda i, meta: (meta[1] * steps + i, 0))
    theirs = pl.BlockSpec((STEP, chans), lambda i, meta: (i, 0))
    return mine, theirs


def fixed(shape):
    return pl.BlockSpec(shape, lambda i, meta: (0,) * len(shape), pipeline_mode=pl.Buffered(1))


def mix_forward(meta, field, other, w_in, w_out, gain):
    cells, chans = other.shape
    hidden = w_in.shape[1]
    mine, theirs = cell_specs(cells, chans)

    def kernel(meta_ref, a_ref, b_ref, wi_ref, wo_ref, gain_ref, own_ref, send_ref):
        x = jnp.concatenate([a_ref[...].astype(F32), b_ref[...].astype(F32)], axis=1)
        y = (layer_norm(x)[0] * gain_ref[...]).astype(BF)
        pre = mxu(y, wi_ref[...])
        tanh = jnp.tanh(pre * (ROOT + (ROOT * CUBIC) * (pre * pre)))
        hid = (pre * (0.5 + 0.5 * tanh)).astype(BF)
        mixed = mxu(hid, wo_ref[...]).astype(BF)
        own_ref[...] = mixed[:, :chans]
        send_ref[...] = mixed[:, chans:]

    return pl.pallas_call(
        kernel,
        grid_spec=pltpu.PrefetchScalarGridSpec(
            num_scalar_prefetch=1,
            grid=(cells // STEP,),
            in_specs=[
                mine,
                theirs,
                fixed((2 * chans, hidden)),
                fixed((hidden, 2 * chans)),
                fixed((1, 2 * chans)),
            ],
            out_specs=[theirs, theirs],
        ),
        out_shape=[jax.ShapeDtypeStruct((cells, chans), BF)] * 2,
        compiler_params=pltpu.CompilerParams(vmem_limit_bytes=48 * 2**20),
        name="mix_forward",
    )(meta, field, other, w_in, w_out, gain)


def mix_backward(meta, field, other, gfield, gother, w_in, w_in_t, w_out_t, gain):
    cells, chans = other.shape
    hidden = w_in.shape[1]
    steps = cells // STEP
    half = hidden // 2
    mine, theirs = cell_specs(cells, chans)

    def kernel(meta_ref, a_ref, b_ref, ga_ref, gb_ref, wi_ref, wit_ref, wot_ref, gain_ref,
               own_ref, send_ref, keep_ref, give_ref, acc_ref):
        i = pl.program_id(0)

        @pl.when(i == 0)
        def _():
            acc_ref[...] = jnp.zeros_like(acc_ref)

        gains = gain_ref[...]
        x = jnp.concatenate([a_ref[...].astype(F32), b_ref[...].astype(F32)], axis=1)
        xhat, inverse = layer_norm(x)
        y = (xhat * gains).astype(BF)
        g = jnp.concatenate([ga_ref[...], gb_ref[...]], axis=1)
        pre = mxu(y, wi_ref[...])
        square = pre * pre
        tanh = jnp.tanh(pre * (ROOT + (ROOT * CUBIC) * square))
        gate = 0.5 + 0.5 * tanh
        act = pre * gate
        slope = gate + (act - act * gate) * (2 * ROOT + (6 * ROOT * CUBIC) * square)
        hid = act.astype(BF)
        dpre = (mxu(g, wot_ref[...]) * slope).astype(BF)
        acc_ref[: 2 * chans] += lax.dot_general(
            y, dpre, (((0,), (0,)), ((), ())), preferred_element_type=F32
        )
        acc_ref[2 * chans :] += lax.dot_general(
            g, hid, (((0,), (0,)), ((), ())), preferred_element_type=F32
        )
        e = mxu(dpre, wit_ref[...]) * gains
        centre = jnp.mean(e, axis=-1, keepdims=True)
        tilt = jnp.mean(e * xhat, axis=-1, keepdims=True)
        dconv = ((e - centre - xhat * tilt) * inverse).astype(BF)
        own_ref[...] = dconv[:, :chans]
        send_ref[...] = dconv[:, chans:]

        @pl.when(i == steps - 1)
        def _():
            me = meta_ref[1]
            for kind in range(2):
                for side in range(2):
                    place = 2 * kind + me + side * (1 - 2 * me)
                    base = (2 * kind + side) * chans
                    keep_ref[place] = acc_ref[base : base + chans, :half]
                    give_ref[place] = acc_ref[base : base + chans, half:].astype(BF)

    grads = pl.BlockSpec((4, chans, half), lambda i, meta: (0, 0, 0))
    return pl.pallas_call(
        kernel,
        grid_spec=pltpu.PrefetchScalarGridSpec(
            num_scalar_prefetch=1,
            grid=(steps,),
            in_specs=[
                mine,
                theirs,
                mine,
                theirs,
                fixed((2 * chans, hidden)),
                fixed((hidden, 2 * chans)),
                fixed((2 * chans, hidden)),
                fixed((1, 2 * chans)),
            ],
            out_specs=[theirs, theirs, grads, grads],
            scratch_shapes=[pltpu.VMEM((4 * chans, hidden), F32)],
        ),
        out_shape=[jax.ShapeDtypeStruct((cells, chans), BF)] * 2
        + [
            jax.ShapeDtypeStruct((4, chans, half), F32),
            jax.ShapeDtypeStruct((4, chans, half), BF),
        ],
        compiler_params=pltpu.CompilerParams(vmem_limit_bytes=56 * 2**20),
        name="mix_backward",
    )(meta, field, other, gfield, gother, w_in, w_in_t, w_out_t, gain)


def lon_halo(block):
    count = lax.axis_size("lon")
    forward = [(i, (i + 1) % count) for i in range(count)]
    backward = [(target, source) for source, target in forward]
    size = block.shape[1]
    low = lax.ppermute(block[:, size - 12 :], "lon", forward)
    high = lax.ppermute(block[:, :12], "lon", backward)
    return low, high


def lat_halo(block, low, high):
    count = lax.axis_size("lat")
    index = lax.axis_index("lat")
    rows = block.shape[0]

    def strip(first):
        parts = [low, block, high]
        return jnp.concatenate(
            [lax.dynamic_slice_in_dim(x, first, 12, 0) for x in parts], axis=1
        )

    if count == 1:
        return []
    if count == 2:
        got = lax.ppermute(strip((1 - index) * (rows - 12)), "lat", [(0, 1), (1, 0)])
        return [((index == 0).astype(jnp.int32), got)]
    down = [(i, i + 1) for i in range(count - 1)]
    up = [(target, source) for source, target in down]
    above = lax.ppermute(strip(rows - 12), "lat", down)
    below = lax.ppermute(strip(0), "lat", up)
    return [(jnp.int32(0), above), (jnp.int32(1), below)]


def halos(block):
    low, high = lon_halo(block)
    return low, high, lat_halo(block, low, high)


def convolve(me, block, halo, weights, base=None):
    low, high, gots = halo
    sums = conv_local(block, low, high, weights)
    if not gots:
        gots = [(jnp.int32(0), jnp.zeros((12, block.shape[1] + 24, block.shape[2]), BF))]
    for n, (below, got) in enumerate(gots):
        last = n == len(gots) - 1
        meta = jnp.stack([below, me])
        sums = conv_remote(meta, sums, got, weights, base if last else None, last)
    return sums


def swap(x):
    return lax.ppermute(x, "ch", [(0, 1), (1, 0)])


def flat(x):
    return x.reshape(-1, x.shape[-1])


def grid_sum(part):
    lon = lax.axis_size("lon")
    lat = lax.axis_size("lat")
    along = [("lon", 2**n) for n in range(lon.bit_length() - 1)]
    across = [("lat", 2**n) for n in range(lat.bit_length() - 1)]
    steps = along[:1] + across + along[1:]

    def partner(x, axis, dist):
        count = lax.axis_size(axis)
        return lax.ppermute(x, axis, [(i, i ^ dist) for i in range(count)])

    for axis, dist in steps:
        bit = (lax.axis_index(axis) // dist) % 2
        half = part.shape[0] // 2
        keep = lax.dynamic_slice_in_dim(part, bit * half, half, 0)
        send = lax.dynamic_slice_in_dim(part, (1 - bit) * half, half, 0)
        part = keep + partner(send.astype(BF), axis, dist).astype(F32)
    part = part.astype(BF)
    for axis, dist in reversed(steps):
        bit = (lax.axis_index(axis) // dist) % 2
        got = partner(part, axis, dist)
        part = jnp.where(bit == 0, jnp.concatenate([part, got]), jnp.concatenate([got, part]))
    return part


def on_device(inputs, cotangent, kernels, gains, w_in, w_out):
    rows, breadth, own = inputs.shape
    cells = rows * breadth // 2
    scaling = 1.0 / math.sqrt(
        rows * lax.axis_size("lat") * breadth * lax.axis_size("lon")
    )
    me = lax.axis_index("ch")
    place = jnp.stack([me, me])

    def own_first(x, axis):
        half = x.shape[axis] // 2
        first = lax.dynamic_slice_in_dim(x, me * half, half, axis)
        second = lax.dynamic_slice_in_dim(x, (1 - me) * half, half, axis)
        return jnp.concatenate([first, second], axis)

    halo0 = halos(inputs)
    w_in_full = own_first(jnp.concatenate([w_in, swap(w_in)], axis=2), 1)
    w_out_full = own_first(jnp.concatenate([w_out, swap(w_out)], axis=1), 2)
    w_in_t = w_in_full.transpose(0, 2, 1)
    w_out_t = w_out_full.transpose(0, 2, 1)
    gains_full = own_first(gains, 1)
    taps = kernels.astype(F32)
    taps_back = taps[:, ::-1]

    def split(field):
        send = lax.dynamic_slice_in_dim(field, (1 - me) * (rows // 2), rows // 2, 0)
        return flat(field), swap(flat(send))

    def join(mine, send):
        theirs = swap(send)
        pair = jnp.where(
            me == 0, jnp.concatenate([mine, theirs]), jnp.concatenate([theirs, mine])
        )
        return pair.reshape(rows, breadth, own)

    def forward(b, block, halo):
        field, send = convolve(me, block, halo, taps[b])
        return flat(field), swap(flat(send))

    def backward(b, conv, grad):
        mine, send, keep, give = mix_backward(
            place, *conv, *grad, w_in_full[b], w_in_t[b], w_out_t[b], gains_full[b : b + 1]
        )
        return join(mine, send), keep, give

    def weight_sums(keep, give):
        half = keep.shape[-1]
        part = keep.reshape(-1, half) + swap(give).reshape(-1, half).astype(F32)
        summed = grid_sum(part).astype(F32) * scaling
        return summed[: 2 * own], summed[2 * own :].T

    def kernel_sums(grad, block, halo):
        low, high, gots = halo
        meta = jnp.stack([below for below, _ in gots] + [me])
        dk = tap_sums(meta, grad, block, low, high, [got for _, got in gots])
        dk = jnp.pad(dk, ((0, 64 - dk.shape[0]), (0, 0)))
        return grid_sum(dk)[:49].astype(F32) * scaling

    conv0 = forward(0, inputs, halo0)
    grad2 = split(cotangent)
    mixed = mix_forward(place, *conv0, w_in_full[0], w_out_full[0], gains_full[:1])
    current = (inputs.astype(F32) + join(*mixed).astype(F32)).astype(BF)
    halo1 = halos(current)
    conv1 = forward(1, current, halo1)

    dconv1, keep1, give1 = backward(1, conv1, grad2)
    back1 = halos(dconv1)
    gwi1, gwo1 = weight_sums(keep1, give1)
    gk1 = kernel_sums(dconv1, current, halo1)
    grad1, send1 = convolve(me, dconv1, back1, taps_back[1], cotangent)
    dconv0, keep0, give0 = backward(0, conv0, (flat(grad1), swap(flat(send1))))
    back0 = halos(dconv0)
    gwi0, gwo0 = weight_sums(keep0, give0)
    gk0 = kernel_sums(dconv0, inputs, halo0)
    grad0, _ = convolve(me, dconv0, back0, taps_back[0], grad1)
    return (grad0, jnp.stack([gwi0, gwi1]), jnp.stack([gwo0, gwo1]), jnp.stack([gk0, gk1]))


def solution(mesh):
    return jax.shard_map(
        on_device,
        mesh=mesh,
        in_specs=(
            P(("grp", "lat"), "lon", "ch"),
            P(("grp", "lat"), "lon", "ch"),
            P(None, None, "ch"),
            P(),
            P(None, None, "ch"),
            P(None, "ch", None),
        ),
        out_specs=(
            P(("grp", "lat"), "lon", "ch"),
            P("grp", None, "ch"),
            P("grp", "ch", None),
            P("grp", None, "ch"),
        ),
        check_vma=False,
    )
```

```python
import math

import jax
import jax.numpy as jnp
from jax import lax
from jax.experimental import pallas as pl
from jax.experimental.pallas import tpu as pltpu
from jax.sharding import PartitionSpec as P

BF = jnp.bfloat16
F32 = jnp.float32


TILE = 32


def cost(us):
    return pl.CostEstimate(flops=int(us * 1e9), transcendentals=0, bytes_accessed=1 << 20)


def call(kernel, us, **kwargs):
    return pl.pallas_call(
        kernel,
        cost_estimate=cost(us),
        compiler_params=pltpu.CompilerParams(vmem_limit_bytes=48 * 2**20),
        **kwargs,
    )


VM = pl.BlockSpec(memory_space=pltpu.VMEM)
SM = pl.BlockSpec(memory_space=pltpu.SMEM)


def spread(wide, shifted, rows, pieces):
    for first, value in pieces:
        wide[:, first : first + value.shape[1], :] = value[...].astype(F32)
    shifted[...] = wide[:, 4 : 4 + shifted.shape[1], :]


def window(wide, shifted, row, tile, col_tap, cols):
    if col_tap % 2:
        return wide[row, pl.ds(pl.multiple_of(tile * cols + 4 * col_tap + 4, 8), cols), :]
    return shifted[row, pl.ds(pl.multiple_of(tile * cols + 4 * col_tap, 8), cols), :]


def wide_shapes(rows, breadth):
    return [pltpu.VMEM((rows, breadth + 32, 128), F32), pltpu.VMEM((rows, breadth + 24, 128), F32)]


def conv_local(block, low, high, weights):
    rows, breadth, chans = block.shape
    groups = rows // 4

    def kernel(block_ref, low_ref, high_ref, w_ref, out_ref, wide, shifted):
        spread(wide, shifted, rows, ((16, block_ref), (4, low_ref), (16 + breadth, high_ref)))
        tiles = breadth // TILE

        def step(i, carry):
            cls, tile = i // tiles, i % tiles
            sums = [jnp.zeros((TILE // 8, 8, chans), F32) for _ in range(groups)]
            for q in range(7):
                taps = {}
                for r in range(groups):
                    v = window(wide, shifted, 4 * r + cls, tile, q, TILE).reshape(-1, 8, chans)
                    for k in range(groups):
                        p = r - k + 3
                        if 0 <= p <= 6:
                            if p not in taps:
                                taps[p] = w_ref[7 * p + q : 7 * p + q + 1, :]
                            sums[k] = sums[k] + taps[p] * v
            for k in range(groups):
                out_ref[4 * k + cls, pl.ds(pl.multiple_of(tile * TILE, 8), TILE), :] = sums[
                    k
                ].reshape(TILE, chans)
            return carry

        lax.fori_loop(0, 4 * tiles, step, 0)

    return call(
        kernel,
        2.5,
        in_specs=[VM] * 4,
        out_specs=VM,
        out_shape=jax.ShapeDtypeStruct(block.shape, F32),
        scratch_shapes=wide_shapes(rows, breadth),
        name="conv_local",
    )(block, low, high, weights)


def conv_remote(meta, sums_in, got, weights, base=None, last=True):
    rows, breadth, chans = sums_in.shape
    groups = rows // 4
    half = rows // 2

    def kernel(meta_ref, sums_ref, got_ref, w_ref, *rest):
        if base is not None:
            base_ref, rest = rest[0], rest[1:]
        if last:
            out_ref, send_ref, wide, shifted = rest
        else:
            out_ref, wide, shifted = rest
        below = meta_ref[0]
        spread(wide, shifted, 12, ((4, got_ref),))
        tiles = breadth // TILE

        def mirror(x, most):
            return x + below * (most - 2 * x)

        def step(i, carry):
            cls, tile = i // tiles, i % tiles
            cols = pl.ds(pl.multiple_of(tile * TILE, 8), TILE)
            at = [4 * mirror(k, groups - 1) + cls for k in range(groups)]
            sums = [sums_ref[at[k], cols, :].reshape(-1, 8, chans) for k in range(groups)]
            for q in range(7):
                taps = [w_ref[pl.ds(7 * mirror(p, 6) + q, 1), :] for p in range(3)]
                for r in range(3):
                    v = window(wide, shifted, 4 * mirror(r, 2) + cls, tile, q, TILE)
                    v = v.reshape(-1, 8, chans)
                    for k in range(min(groups, r + 1)):
                        sums[k] = sums[k] + taps[r - k] * v
            for k in range(groups):
                value = sums[k].reshape(TILE, chans)
                if base is not None:
                    value = value + base_ref[at[k], cols, :].astype(F32)
                out_ref[at[k], cols, :] = value.astype(out_ref.dtype)
            return carry

        lax.fori_loop(0, 4 * tiles, step, 0)
        if last:
            send_ref[...] = out_ref[pl.ds((1 - meta_ref[1]) * half, half)]

    field = jax.ShapeDtypeStruct((rows, breadth, chans), BF if last else F32)
    part = jax.ShapeDtypeStruct((half, breadth, chans), BF)
    args = (meta, sums_in, got, weights) + (() if base is None else (base,))
    return call(
        kernel,
        1.7,
        in_specs=[SM] + [VM] * (len(args) - 1),
        out_specs=(VM, VM) if last else VM,
        out_shape=(field, part) if last else field,
        scratch_shapes=wide_shapes(12, breadth),
        name="conv_remote",
    )(*args)


def tap_sums(meta, grad, block, low, high, gots):
    rows, breadth, chans = block.shape
    groups = rows // 4
    count = len(gots)

    def kernel(meta_ref, grad_ref, block_ref, low_ref, high_ref, *rest):
        got_refs, (packed_ref, out_ref, g_ref, wide, shifted, rwide, rshifted) = (
            rest[:count],
            rest[count:],
        )
        out_ref[48:] = jnp.zeros((16, chans), F32)
        g_ref[...] = grad_ref[...].astype(F32)
        spread(wide, shifted, rows, ((16, block_ref), (4, low_ref), (16 + breadth, high_ref)))
        tiles = breadth // 8

        def near(cols_taps):
            def step(i, sums):
                cls, tile = i // tiles, i % tiles
                sums = list(sums)
                cols = pl.ds(pl.multiple_of(tile * 8, 8), 8)
                g = [g_ref[4 * k + cls, cols, :] for k in range(groups)]
                for n, q in enumerate(cols_taps):
                    for r in range(groups):
                        v = window(wide, shifted, 4 * r + cls, tile, q, 8)
                        for k in range(groups):
                            p = r - k + 3
                            if 0 <= p <= 6:
                                sums[7 * n + p] = sums[7 * n + p] + g[k] * v
                return tuple(sums)

            zero = jnp.zeros((8, chans), F32)
            sums = lax.fori_loop(0, 4 * tiles, step, (zero,) * (7 * len(cols_taps)))
            for n, q in enumerate(cols_taps):
                for p in range(7):
                    out_ref[7 * p + q : 7 * p + q + 1, :] = jnp.sum(
                        sums[7 * n + p], axis=0, keepdims=True
                    )

        def far(index, cols_taps):
            below = meta_ref[index]

            def mirror(x, most):
                return x + below * (most - 2 * x)

            def step(i, sums):
                cls, tile = i // tiles, i % tiles
                sums = list(sums)
                cols = pl.ds(pl.multiple_of(tile * 8, 8), 8)
                near_k = range(min(3, groups))
                g = [g_ref[4 * mirror(k, groups - 1) + cls, cols, :] for k in near_k]
                for n, q in enumerate(cols_taps):
                    for r in range(3):
                        v = window(rwide, rshifted, 4 * mirror(r, 2) + cls, tile, q, 8)
                        for k in near_k:
                            if k <= r:
                                sums[3 * n + r - k] = sums[3 * n + r - k] + g[k] * v
                return tuple(sums)

            zero = jnp.zeros((8, chans), F32)
            sums = lax.fori_loop(0, 4 * tiles, step, (zero,) * (3 * len(cols_taps)))
            for n, q in enumerate(cols_taps):
                for p in range(3):
                    at = pl.ds(7 * mirror(p, 6) + q, 1)
                    out_ref[at, :] = out_ref[at, :] + jnp.sum(
                        sums[3 * n + p], axis=0, keepdims=True
                    )

        for cols_taps in ((0, 2, 4, 6), (1, 3, 5)):
            near(cols_taps)
        for index in range(count):
            spread(rwide, rshifted, 12, ((4, got_refs[index]),))
            far(index, tuple(range(7)))
        for lane in range(4):
            packed_ref[:, lane * chans : (lane + 1) * chans] = out_ref[pl.ds(lane, 16, stride=4), :]

    return call(
        kernel,
        6.8,
        in_specs=[SM] + [VM] * (4 + count),
        out_specs=VM,
        out_shape=jax.ShapeDtypeStruct((16, 4 * chans), F32),
        scratch_shapes=[pltpu.VMEM((64, chans), F32), pltpu.VMEM(block.shape, F32)]
        + wide_shapes(rows, breadth)
        + wide_shapes(12, breadth),
        name="tap_sums",
    )(meta, grad, block, low, high, *gots)


CUBIC = 0.044715
ROOT = math.sqrt(2.0 / math.pi)


def layer_norm(x):
    centred = x - jnp.mean(x, axis=-1, keepdims=True)
    inverse = lax.rsqrt(jnp.mean(centred * centred, axis=-1, keepdims=True) + 1e-06)
    return centred * inverse, inverse


def mxu(a, b):
    return jnp.dot(a, b, preferred_element_type=F32)


STEP = 256


def cell_specs(cells, chans):
    steps = cells // STEP
    mine = pl.BlockSpec((STEP, chans), lambda i, meta: (meta[1] * steps + i, 0))
    theirs = pl.BlockSpec((STEP, chans), lambda i, meta: (i, 0))
    return mine, theirs


def fixed(shape):
    return pl.BlockSpec(shape, lambda i, meta: (0,) * len(shape), pipeline_mode=pl.Buffered(1))


def natural(me, a, b):
    first = me == 0
    return jnp.concatenate([jnp.where(first, a, b), jnp.where(first, b, a)], axis=1)


def deal(me, x, own_ref, send_ref):
    chans = x.shape[1] // 2
    left, right = x[:, :chans], x[:, chans:]
    own_ref[...] = jnp.where(me == 0, left, right).astype(BF)
    send_ref[...] = jnp.where(me == 0, right, left).astype(BF)


def fold(a, b, left, right):
    return lax.dot_general(a, b, (((left,), (right,)), ((), ())), preferred_element_type=F32)


def weight_specs(b, w_in, w_out, gains):
    wi = pl.BlockSpec((1,) + w_in.shape[1:], lambda i, meta: (b, 0, 0), pipeline_mode=pl.Buffered(1))
    wo = pl.BlockSpec((1,) + w_out.shape[1:], lambda i, meta: (b, 0, 0), pipeline_mode=pl.Buffered(1))
    return [wi, wi, wo, wo, fixed(gains.shape)]


def mix_forward(b, meta, field, other, weights):
    cells, chans = other.shape
    mine, theirs = cell_specs(cells, chans)

    def kernel(meta_ref, a_ref, b_ref, wi0, wi1, wo0, wo1, gain_ref, own_ref, send_ref):
        me = meta_ref[1]
        x = natural(me, a_ref[...].astype(F32), b_ref[...].astype(F32))
        y = (layer_norm(x)[0] * gain_ref[b : b + 1]).astype(BF)
        mixed = None
        for wi, wo in ((wi0, wo0), (wi1, wo1)):
            pre = mxu(y, wi[0])
            tanh = jnp.tanh(pre * (ROOT + (ROOT * CUBIC) * (pre * pre)))
            hid = (pre * (0.5 + 0.5 * tanh)).astype(BF)
            part = mxu(hid, wo[0])
            mixed = part if mixed is None else mixed + part
        deal(me, mixed, own_ref, send_ref)

    return pl.pallas_call(
        kernel,
        grid_spec=pltpu.PrefetchScalarGridSpec(
            num_scalar_prefetch=1,
            grid=(cells // STEP,),
            in_specs=[mine, theirs] + weight_specs(b, weights[0], weights[2], weights[4]),
            out_specs=[theirs, theirs],
        ),
        out_shape=[jax.ShapeDtypeStruct((cells, chans), BF)] * 2,
        cost_estimate=cost(4),
        compiler_params=pltpu.CompilerParams(vmem_limit_bytes=48 * 2**20),
        name="mix_forward",
    )(meta, field, other, *weights)


def mix_backward(b, meta, field, other, gfield, gother, weights, pieces):
    cells, chans = other.shape
    steps = cells // STEP
    half = weights[0].shape[2]
    size = 4 * chans // pieces
    mine, theirs = cell_specs(cells, chans)

    def kernel(meta_ref, a_ref, b_ref, ga_ref, gb_ref, wi0, wi1, wo0, wo1, gain_ref,
               own_ref, send_ref, keep_ref, give_ref, acc_ref):
        i = pl.program_id(0)
        me = meta_ref[1]

        @pl.when(i == 0)
        def _():
            acc_ref[...] = jnp.zeros_like(acc_ref)

        gains = gain_ref[b : b + 1]
        x = natural(me, a_ref[...].astype(F32), b_ref[...].astype(F32))
        xhat, inverse = layer_norm(x)
        y = (xhat * gains).astype(BF)
        g = natural(me, ga_ref[...], gb_ref[...])
        dy = None
        for n, (wi, wo) in enumerate(((wi0, wo0), (wi1, wo1))):
            pre = mxu(y, wi[0])
            square = pre * pre
            tanh = jnp.tanh(pre * (ROOT + (ROOT * CUBIC) * square))
            gate = 0.5 + 0.5 * tanh
            act = pre * gate
            slope = gate + (act - act * gate) * (2 * ROOT + (6 * ROOT * CUBIC) * square)
            hid = act.astype(BF)
            dpre = (fold(g, wo[0], 1, 1) * slope).astype(BF)
            acc_ref[n, : 2 * chans] += fold(y, dpre, 0, 0)
            acc_ref[n, 2 * chans :] += fold(g, hid, 0, 0)
            part = fold(dpre, wi[0], 1, 1)
            dy = part if dy is None else dy + part
        e = dy * gains
        centre = jnp.mean(e, axis=-1, keepdims=True)
        tilt = jnp.mean(e * xhat, axis=-1, keepdims=True)
        deal(me, (e - centre - xhat * tilt) * inverse, own_ref, send_ref)

        @pl.when(i == steps - 1)
        def _():
            bits = meta_ref[2]
            for p in range(pieces):
                rows = slice(p * size, (p + 1) * size)
                keep_ref[p ^ bits] = acc_ref[0, rows]
                give_ref[p ^ bits] = acc_ref[1, rows].astype(BF)

    grads = pl.BlockSpec((pieces, size, half), lambda i, meta: (0, 0, 0))
    return pl.pallas_call(
        kernel,
        grid_spec=pltpu.PrefetchScalarGridSpec(
            num_scalar_prefetch=1,
            grid=(steps,),
            in_specs=[mine, theirs, mine, theirs]
            + weight_specs(b, weights[0], weights[2], weights[4]),
            out_specs=[theirs, theirs, grads, grads],
            scratch_shapes=[pltpu.VMEM((2, 4 * chans, half), F32)],
        ),
        out_shape=[jax.ShapeDtypeStruct((cells, chans), BF)] * 2
        + [
            jax.ShapeDtypeStruct((pieces, size, half), F32),
            jax.ShapeDtypeStruct((pieces, size, half), BF),
        ],
        cost_estimate=cost(9),
        compiler_params=pltpu.CompilerParams(vmem_limit_bytes=56 * 2**20),
        name="mix_backward",
    )(meta, field, other, gfield, gother, *weights)


def unpack(b, meta, mine, got, scaling, pieces, earlier=None):
    size, half = 2 * mine.shape[0] // pieces, mine.shape[1]
    chans = pieces * size // 2

    def kernel(meta_ref, mine_ref, got_ref, *rest):
        first_ref, second_ref, flip_ref = rest[-3:]
        bits = meta_ref[2]
        for r in range(pieces):
            source = mine_ref if r < pieces // 2 else got_ref
            at = (r % (pieces // 2)) * size
            value = source[at : at + size, :].astype(F32) * scaling
            flip_ref[r ^ bits] = value
        per = pieces // 2
        for p in range(per):
            first_ref[0, p * size : (p + 1) * size, :] = flip_ref[p]
        second_ref[0] = flip_ref[per:].reshape(chans, half).T

    outs = (
        jax.ShapeDtypeStruct((2, chans, half), F32),
        jax.ShapeDtypeStruct((2, half, chans), F32),
    )
    earlier = () if earlier is None else tuple(earlier)
    return pl.pallas_call(
        kernel,
        grid=(1,),
        in_specs=[SM, VM, VM] + [pl.BlockSpec(memory_space=pl.ANY)] * len(earlier),
        out_specs=(
            pl.BlockSpec((1, chans, half), lambda i: (b, 0, 0)),
            pl.BlockSpec((1, half, chans), lambda i: (b, 0, 0)),
        ),
        out_shape=outs,
        scratch_shapes=[pltpu.VMEM((pieces, size, half), F32)],
        input_output_aliases={3 + n: n for n in range(len(earlier))},
        cost_estimate=cost(1.5),
        compiler_params=pltpu.CompilerParams(vmem_limit_bytes=48 * 2**20),
        name="unpack",
    )(meta, mine, got, *earlier)


def lon_halo(block):
    count = lax.axis_size("lon")
    forward = [(i, (i + 1) % count) for i in range(count)]
    backward = [(target, source) for source, target in forward]
    size = block.shape[1]
    low = lax.ppermute(block[:, size - 12 :], "lon", forward)
    high = lax.ppermute(block[:, :12], "lon", backward)
    return low, high


def lat_halo(block, low, high):
    count = lax.axis_size("lat")
    index = lax.axis_index("lat")
    rows = block.shape[0]

    def strip(first):
        parts = [low, block, high]
        return jnp.concatenate(
            [lax.dynamic_slice_in_dim(x, first, 12, 0) for x in parts], axis=1
        )

    if count == 1:
        return []
    if count == 2:
        got = lax.ppermute(strip((1 - index) * (rows - 12)), "lat", [(0, 1), (1, 0)])
        return [((index == 0).astype(jnp.int32), got)]
    down = [(i, i + 1) for i in range(count - 1)]
    up = [(target, source) for source, target in down]
    above = lax.ppermute(strip(rows - 12), "lat", down)
    below = lax.ppermute(strip(0), "lat", up)
    return [(jnp.int32(0), above), (jnp.int32(1), below)]


def halos(block):
    low, high = lon_halo(block)
    return low, high, lat_halo(block, low, high)


def convolve(me, block, halo, weights, base=None):
    low, high, gots = halo
    sums = conv_local(block, low, high, weights)
    if not gots:
        gots = [(jnp.int32(0), jnp.zeros((12, block.shape[1] + 24, block.shape[2]), BF))]
    for n, (below, got) in enumerate(gots):
        last = n == len(gots) - 1
        meta = jnp.stack([below, me])
        sums = conv_remote(meta, sums, got, weights, base if last else None, last)
    return sums


def swap(x):
    return lax.ppermute(x, "ch", [(0, 1), (1, 0)])


def flat(x):
    return x.reshape(-1, x.shape[-1])


def exchanges():
    lon = lax.axis_size("lon")
    lat = lax.axis_size("lat")
    along = [("lon", 2**n) for n in range(lon.bit_length() - 1)]
    across = [("lat", 2**n) for n in range(lat.bit_length() - 1)]
    return along[:1] + across + along[1:]


def partner(x, axis, dist):
    count = lax.axis_size(axis)
    return lax.ppermute(x, axis, [(i, i ^ dist) for i in range(count)])


def scatter_sum(part):
    for axis, dist in exchanges():
        half = part.shape[0] // 2
        part = part[:half] + partner(part[half:].astype(BF), axis, dist).astype(F32)
    return part.astype(BF)


def gather(part, extra=None):
    got = None
    for axis, dist in reversed(exchanges()):
        if got is not None:
            part = jnp.concatenate([part, got])
        rows = part.shape[0]
        if extra is None:
            got = partner(part, axis, dist)
        else:
            both = partner(jnp.concatenate([part, extra.astype(BF)]), axis, dist)
            got = both[:rows]
            extra = extra.astype(BF).astype(F32) + both[rows:].astype(F32)
    return part, got, extra


def on_device(inputs, cotangent, kernels, gains, w_in, w_out):
    rows, breadth, own = inputs.shape
    scaling = 1.0 / math.sqrt(
        rows * lax.axis_size("lat") * breadth * lax.axis_size("lon")
    )
    me = lax.axis_index("ch")
    steps = exchanges()
    pieces = 2 ** len(steps)
    bits = 0
    for axis, dist in steps:
        bits = 2 * bits + (lax.axis_index(axis) // dist) % 2
    place = jnp.stack([me, me, bits])

    halo0 = halos(inputs)
    weights = (w_in, swap(w_in), w_out, swap(w_out), gains)
    taps = kernels.astype(F32)
    taps_back = taps[:, ::-1]

    def split(field):
        send = lax.dynamic_slice_in_dim(field, (1 - me) * (rows // 2), rows // 2, 0)
        return flat(field), swap(flat(send))

    def join(mine, send):
        theirs = swap(send)
        pair = jnp.where(
            me == 0, jnp.concatenate([mine, theirs]), jnp.concatenate([theirs, mine])
        )
        return pair.reshape(rows, breadth, own)

    def forward(b, block, halo):
        field, send = convolve(me, block, halo, taps[b])
        return flat(field), swap(flat(send))

    def scattered(keep, give):
        return scatter_sum(flat(keep) + swap(flat(give)).astype(F32))

    def kernel_sums(grad, block, halo):
        low, high, gots = halo
        meta = jnp.stack([below for below, _ in gots] + [me])
        return tap_sums(meta, grad, block, low, high, [got for _, got in gots])

    def backward(b, conv, grad, block, halo, base):
        mine, send, keep, give = mix_backward(b, place, *conv, *grad, weights, pieces)
        dconv = join(mine, send)
        back = halos(dconv)
        late, _, _ = lax.optimization_barrier((dconv, back[0], back[1]))
        dk = kernel_sums(late, block, halo)
        field, send = convolve(me, dconv, back, taps_back[b], base)
        return field, send, scattered(keep, give), dk

    conv0 = forward(0, inputs, halo0)
    grad2 = split(cotangent)
    mixed = mix_forward(0, place, *conv0, weights)
    current = (inputs.astype(F32) + join(*mixed).astype(F32)).astype(BF)
    halo1 = halos(current)
    conv1 = forward(1, current, halo1)
    grad1, send1, sums1, dk1 = backward(1, conv1, grad2, current, halo1, cotangent)
    swapped = (flat(grad1), swap(flat(send1)))
    grad0, _, sums0, dk0 = backward(0, conv0, swapped, inputs, halo0, grad1)

    part1, got1, _ = gather(sums1)
    outs = unpack(1, place, part1, got1, scaling, pieces)
    part0, got0, dk = gather(sums0, jnp.concatenate([dk0, dk1]))
    outs = unpack(0, place, part0, got0, scaling, pieces, outs)
    dk = dk.reshape(2, -1, own)[:, :49] * scaling
    return grad0, outs[0], outs[1], dk


def solution(mesh):
    return jax.shard_map(
        on_device,
        mesh=mesh,
        in_specs=(
            P(("grp", "lat"), "lon", "ch"),
            P(("grp", "lat"), "lon", "ch"),
            P(None, None, "ch"),
            P(),
            P(None, None, "ch"),
            P(None, "ch", None),
        ),
        out_specs=(
            P(("grp", "lat"), "lon", "ch"),
            P("grp", None, "ch"),
            P("grp", "ch", None),
            P("grp", None, "ch"),
        ),
        check_vma=False,
    )
```

```python
import math

import jax
import jax.numpy as jnp
from jax import lax
from jax.experimental import pallas as pl
from jax.experimental.pallas import tpu as pltpu
from jax.sharding import PartitionSpec as P

BF = jnp.bfloat16
F32 = jnp.float32


TILE = 32


def cost(us):
    return pl.CostEstimate(flops=int(us * 1e9), transcendentals=0, bytes_accessed=1 << 20)


def call(kernel, us, grant, **kwargs):
    return pl.pallas_call(
        kernel,
        cost_estimate=cost(us),
        compiler_params=pltpu.CompilerParams(vmem_limit_bytes=grant * 2**20),
        **kwargs,
    )


VM = pl.BlockSpec(memory_space=pltpu.VMEM)
SM = pl.BlockSpec(memory_space=pltpu.SMEM)


def spread(wide, shifted, rows, pieces):
    for first, value in pieces:
        wide[:, first : first + value.shape[1], :] = value[...].astype(F32)
    shifted[...] = wide[:, 4 : 4 + shifted.shape[1], :]


def window(wide, shifted, row, tile, col_tap, cols):
    if col_tap % 2:
        return wide[row, pl.ds(pl.multiple_of(tile * cols + 4 * col_tap + 4, 8), cols), :]
    return shifted[row, pl.ds(pl.multiple_of(tile * cols + 4 * col_tap, 8), cols), :]


def wide_shapes(rows, breadth):
    return [pltpu.VMEM((rows, breadth + 32, 128), F32), pltpu.VMEM((rows, breadth + 24, 128), F32)]


def conv_local(block, low, high, weights):
    rows, breadth, chans = block.shape
    groups = rows // 4

    def kernel(block_ref, low_ref, high_ref, w_ref, out_ref, wide, shifted):
        spread(wide, shifted, rows, ((16, block_ref), (4, low_ref), (16 + breadth, high_ref)))
        tiles = breadth // TILE

        def step(i, carry):
            cls, tile = i // tiles, i % tiles
            sums = [jnp.zeros((TILE // 8, 8, chans), F32) for _ in range(groups)]
            for q in range(7):
                taps = {}
                for r in range(groups):
                    v = window(wide, shifted, 4 * r + cls, tile, q, TILE).reshape(-1, 8, chans)
                    for k in range(groups):
                        p = r - k + 3
                        if 0 <= p <= 6:
                            if p not in taps:
                                taps[p] = w_ref[7 * p + q : 7 * p + q + 1, :]
                            sums[k] = sums[k] + taps[p] * v
            for k in range(groups):
                out_ref[4 * k + cls, pl.ds(pl.multiple_of(tile * TILE, 8), TILE), :] = sums[
                    k
                ].reshape(TILE, chans)
            return carry

        lax.fori_loop(0, 4 * tiles, step, 0)

    return call(
        kernel,
        2.5,
        8,
        in_specs=[VM] * 4,
        out_specs=VM,
        out_shape=jax.ShapeDtypeStruct(block.shape, F32),
        scratch_shapes=wide_shapes(rows, breadth),
        name="conv_local",
    )(block, low, high, weights)


def conv_remote(meta, sums_in, got, weights, base=None, last=True):
    rows, breadth, chans = sums_in.shape
    groups = rows // 4
    half = rows // 2

    def kernel(meta_ref, sums_ref, got_ref, w_ref, *rest):
        if base is not None:
            base_ref, rest = rest[0], rest[1:]
        if last:
            out_ref, send_ref, wide, shifted = rest
        else:
            out_ref, wide, shifted = rest
        below = meta_ref[0]
        spread(wide, shifted, 12, ((4, got_ref),))
        tiles = breadth // TILE

        def mirror(x, most):
            return x + below * (most - 2 * x)

        def step(i, carry):
            cls, tile = i // tiles, i % tiles
            cols = pl.ds(pl.multiple_of(tile * TILE, 8), TILE)
            at = [4 * mirror(k, groups - 1) + cls for k in range(groups)]
            sums = [sums_ref[at[k], cols, :].reshape(-1, 8, chans) for k in range(groups)]
            for q in range(7):
                taps = [w_ref[pl.ds(7 * mirror(p, 6) + q, 1), :] for p in range(3)]
                for r in range(3):
                    v = window(wide, shifted, 4 * mirror(r, 2) + cls, tile, q, TILE)
                    v = v.reshape(-1, 8, chans)
                    for k in range(min(groups, r + 1)):
                        sums[k] = sums[k] + taps[r - k] * v
            for k in range(groups):
                value = sums[k].reshape(TILE, chans)
                if base is not None:
                    value = value + base_ref[at[k], cols, :].astype(F32)
                out_ref[at[k], cols, :] = value.astype(out_ref.dtype)
            return carry

        lax.fori_loop(0, 4 * tiles, step, 0)
        if last:
            send_ref[...] = out_ref[pl.ds((1 - meta_ref[1]) * half, half)]

    field = jax.ShapeDtypeStruct((rows, breadth, chans), BF if last else F32)
    part = jax.ShapeDtypeStruct((half, breadth, chans), BF)
    args = (meta, sums_in, got, weights) + (() if base is None else (base,))
    return call(
        kernel,
        1.7,
        10,
        in_specs=[SM] + [VM] * (len(args) - 1),
        out_specs=(VM, VM) if last else VM,
        out_shape=(field, part) if last else field,
        scratch_shapes=wide_shapes(12, breadth),
        name="conv_remote",
    )(*args)


def tap_sums(meta, grad, block, low, high, gots):
    rows, breadth, chans = block.shape
    groups = rows // 4
    count = len(gots)

    def kernel(meta_ref, grad_ref, block_ref, low_ref, high_ref, *rest):
        got_refs, (packed_ref, out_ref, g_ref, wide, shifted, rwide, rshifted) = (
            rest[:count],
            rest[count:],
        )
        out_ref[48:] = jnp.zeros((16, chans), F32)
        g_ref[...] = grad_ref[...].astype(F32)
        spread(wide, shifted, rows, ((16, block_ref), (4, low_ref), (16 + breadth, high_ref)))
        tiles = breadth // 8

        def near(cols_taps):
            def step(i, sums):
                cls, tile = i // tiles, i % tiles
                sums = list(sums)
                cols = pl.ds(pl.multiple_of(tile * 8, 8), 8)
                g = [g_ref[4 * k + cls, cols, :] for k in range(groups)]
                for n, q in enumerate(cols_taps):
                    for r in range(groups):
                        v = window(wide, shifted, 4 * r + cls, tile, q, 8)
                        for k in range(groups):
                            p = r - k + 3
                            if 0 <= p <= 6:
                                sums[7 * n + p] = sums[7 * n + p] + g[k] * v
                return tuple(sums)

            zero = jnp.zeros((8, chans), F32)
            sums = lax.fori_loop(0, 4 * tiles, step, (zero,) * (7 * len(cols_taps)))
            for n, q in enumerate(cols_taps):
                for p in range(7):
                    out_ref[7 * p + q : 7 * p + q + 1, :] = jnp.sum(
                        sums[7 * n + p], axis=0, keepdims=True
                    )

        def far(index, cols_taps):
            below = meta_ref[index]

            def mirror(x, most):
                return x + below * (most - 2 * x)

            def step(i, sums):
                cls, tile = i // tiles, i % tiles
                sums = list(sums)
                cols = pl.ds(pl.multiple_of(tile * 8, 8), 8)
                near_k = range(min(3, groups))
                g = [g_ref[4 * mirror(k, groups - 1) + cls, cols, :] for k in near_k]
                for n, q in enumerate(cols_taps):
                    for r in range(3):
                        v = window(rwide, rshifted, 4 * mirror(r, 2) + cls, tile, q, 8)
                        for k in near_k:
                            if k <= r:
                                sums[3 * n + r - k] = sums[3 * n + r - k] + g[k] * v
                return tuple(sums)

            zero = jnp.zeros((8, chans), F32)
            sums = lax.fori_loop(0, 4 * tiles, step, (zero,) * (3 * len(cols_taps)))
            for n, q in enumerate(cols_taps):
                for p in range(3):
                    at = pl.ds(7 * mirror(p, 6) + q, 1)
                    out_ref[at, :] = out_ref[at, :] + jnp.sum(
                        sums[3 * n + p], axis=0, keepdims=True
                    )

        for cols_taps in ((0, 2, 4, 6), (1, 3, 5)):
            near(cols_taps)
        for index in range(count):
            spread(rwide, rshifted, 12, ((4, got_refs[index]),))
            far(index, tuple(range(7)))
        for lane in range(4):
            packed_ref[:, lane * chans : (lane + 1) * chans] = out_ref[pl.ds(lane, 16, stride=4), :]

    return call(
        kernel,
        6.8,
        14,
        in_specs=[SM] + [VM] * (4 + count),
        out_specs=VM,
        out_shape=jax.ShapeDtypeStruct((16, 4 * chans), F32),
        scratch_shapes=[pltpu.VMEM((64, chans), F32), pltpu.VMEM(block.shape, F32)]
        + wide_shapes(rows, breadth)
        + wide_shapes(12, breadth),
        name="tap_sums",
    )(meta, grad, block, low, high, *gots)


CUBIC = 0.044715
ROOT = math.sqrt(2.0 / math.pi)


def layer_norm(x):
    centred = x - jnp.mean(x, axis=-1, keepdims=True)
    inverse = lax.rsqrt(jnp.mean(centred * centred, axis=-1, keepdims=True) + 1e-06)
    return centred * inverse, inverse


def mxu(a, b):
    return jnp.dot(a, b, preferred_element_type=F32)


def cell_specs(cells, chans):
    mine = pl.BlockSpec((cells, chans), lambda i, meta: (meta[1], 0))
    theirs = pl.BlockSpec((cells, chans), lambda i, meta: (0, 0))
    return mine, theirs


def whole(shape):
    return pl.BlockSpec(shape, lambda i, meta: (0,) * len(shape))


def one_step(kernel, us, grant, in_specs, out_specs, out_shape, name, scratch=()):
    return pl.pallas_call(
        kernel,
        grid_spec=pltpu.PrefetchScalarGridSpec(
            num_scalar_prefetch=1,
            grid=(1,),
            in_specs=in_specs,
            out_specs=out_specs,
            scratch_shapes=list(scratch),
        ),
        out_shape=out_shape,
        cost_estimate=cost(us),
        compiler_params=pltpu.CompilerParams(vmem_limit_bytes=grant * 2**20),
        name=name,
    )


def natural(me, a, b):
    first = me == 0
    return jnp.concatenate([jnp.where(first, a, b), jnp.where(first, b, a)], axis=1)


def deal(me, x, own_ref, send_ref):
    chans = x.shape[1] // 2
    left, right = x[:, :chans], x[:, chans:]
    own_ref[...] = jnp.where(me == 0, left, right).astype(BF)
    send_ref[...] = jnp.where(me == 0, right, left).astype(BF)


def fold(a, b, left, right):
    return lax.dot_general(a, b, (((left,), (right,)), ((), ())), preferred_element_type=F32)


def weight_specs(b, weights):
    specs = [
        pl.BlockSpec((1,) + w.shape[1:], lambda i, meta: (b, 0, 0)) for w in weights[:4]
    ]
    return specs + [whole(weights[4].shape)]


CHUNK = 256


def chunks(weights):
    wi0, wi1, wo0, wo1 = weights
    count = wi0.shape[2] // CHUNK
    for n, (wi, wo) in enumerate(((wi0, wo0), (wi1, wo1))):
        for c in range(count):
            at = slice(c * CHUNK, (c + 1) * CHUNK)
            yield n, at, wi[0, :, at], wo[0, at, :]


def mix_forward(b, meta, field, other, weights):
    cells, chans = other.shape
    mine, theirs = cell_specs(cells, chans)

    def kernel(meta_ref, a_ref, b_ref, wi0, wi1, wo0, wo1, gain_ref, own_ref, send_ref):
        me = meta_ref[1]
        x = natural(me, a_ref[...].astype(F32), b_ref[...].astype(F32))
        y = (layer_norm(x)[0] * gain_ref[b : b + 1]).astype(BF)
        mixed = None
        for _, _, wi, wo in chunks((wi0, wi1, wo0, wo1)):
            pre = mxu(y, wi)
            tanh = jnp.tanh(pre * (ROOT + (ROOT * CUBIC) * (pre * pre)))
            hid = (pre * (0.5 + 0.5 * tanh)).astype(BF)
            part = mxu(hid, wo)
            mixed = part if mixed is None else mixed + part
        deal(me, mixed, own_ref, send_ref)

    return one_step(
        kernel,
        4,
        24,
        [mine, theirs] + weight_specs(b, weights),
        [theirs, theirs],
        [jax.ShapeDtypeStruct((cells, chans), BF)] * 2,
        "mix_forward",
    )(meta, field, other, *weights)


def hidden_back(y, g, wi, wo):
    pre = mxu(y, wi)
    square = pre * pre
    tanh = jnp.tanh(pre * (ROOT + (ROOT * CUBIC) * square))
    gate = 0.5 + 0.5 * tanh
    act = pre * gate
    slope = gate + (act - act * gate) * (2 * ROOT + (6 * ROOT * CUBIC) * square)
    return act.astype(BF), (fold(g, wo, 1, 1) * slope).astype(BF)


def norm_back(me, dy, gains, xhat, inverse, own_ref, send_ref):
    e = dy * gains
    centre = jnp.mean(e, axis=-1, keepdims=True)
    tilt = jnp.mean(e * xhat, axis=-1, keepdims=True)
    deal(me, (e - centre - xhat * tilt) * inverse, own_ref, send_ref)


def mix_backward(b, meta, field, other, gfield, gother, weights, pieces, late):
    cells, chans = other.shape
    half = weights[0].shape[2]
    size = 4 * chans // pieces
    mine, theirs = cell_specs(cells, chans)

    def kernel(meta_ref, a_ref, b_ref, ga_ref, gb_ref, wi0, wi1, wo0, wo1, gain_ref, *rest):
        *first, keep_ref, give_ref, acc_ref = rest
        me = meta_ref[1]
        gains = gain_ref[b : b + 1]
        x = natural(me, a_ref[...].astype(F32), b_ref[...].astype(F32))
        xhat, inverse = layer_norm(x)
        y = (xhat * gains).astype(BF)
        g = natural(me, ga_ref[...], gb_ref[...])
        dy = None
        for n, at, wi, wo in chunks((wi0, wi1, wo0, wo1)):
            hid, dpre = hidden_back(y, g, wi, wo)
            acc_ref[n, : 2 * chans, at] = fold(y, dpre, 0, 0)
            acc_ref[n, 2 * chans :, at] = fold(g, hid, 0, 0)
            if late:
                first[0][n, :, at] = dpre
            else:
                part = fold(dpre, wi, 1, 1)
                dy = part if dy is None else dy + part
        if not late:
            norm_back(me, dy, gains, xhat, inverse, *first)
        bits = meta_ref[2]
        for p in range(pieces):
            rows = slice(p * size, (p + 1) * size)
            keep_ref[p ^ bits] = acc_ref[0, rows]
            give_ref[p ^ bits] = acc_ref[1, rows].astype(BF)

    grads = whole((pieces, size, half))
    cell = jax.ShapeDtypeStruct((cells, chans), BF)
    return one_step(
        kernel,
        7 if late else 9,
        36,
        [mine, theirs, mine, theirs] + weight_specs(b, weights),
        ([whole((2, cells, half))] if late else [theirs, theirs]) + [grads, grads],
        ([jax.ShapeDtypeStruct((2, cells, half), BF)] if late else [cell, cell])
        + [
            jax.ShapeDtypeStruct((pieces, size, half), F32),
            jax.ShapeDtypeStruct((pieces, size, half), BF),
        ],
        "mix_weights" if late else "mix_backward",
        [pltpu.VMEM((2, 4 * chans, half), F32)],
    )(meta, field, other, gfield, gother, *weights)


def mix_inputs(b, meta, field, other, dpre, weights):
    cells, chans = other.shape
    mine, theirs = cell_specs(cells, chans)

    def kernel(meta_ref, a_ref, b_ref, dpre_ref, wi0, wi1, gain_ref, own_ref, send_ref):
        me = meta_ref[1]
        x = natural(me, a_ref[...].astype(F32), b_ref[...].astype(F32))
        xhat, inverse = layer_norm(x)
        dy = fold(dpre_ref[0], wi0[0], 1, 1) + fold(dpre_ref[1], wi1[0], 1, 1)
        norm_back(me, dy, gain_ref[b : b + 1], xhat, inverse, own_ref, send_ref)

    specs = weight_specs(b, weights)
    return one_step(
        kernel,
        3,
        24,
        [mine, theirs, whole(dpre.shape), specs[0], specs[1], specs[4]],
        [theirs, theirs],
        [jax.ShapeDtypeStruct((cells, chans), BF)] * 2,
        "mix_inputs",
    )(meta, field, other, dpre, weights[0], weights[1], weights[4])


def unpack(b, meta, mine, got, scaling, pieces, earlier=None):
    size, half = 2 * mine.shape[0] // pieces, mine.shape[1]
    chans = pieces * size // 2

    def kernel(meta_ref, mine_ref, got_ref, *rest):
        first_ref, second_ref, flip_ref = rest[-3:]
        bits = meta_ref[2]
        for r in range(pieces):
            source = mine_ref if r < pieces // 2 else got_ref
            at = (r % (pieces // 2)) * size
            value = source[at : at + size, :].astype(F32) * scaling
            flip_ref[r ^ bits] = value
        per = pieces // 2
        for p in range(per):
            first_ref[0, p * size : (p + 1) * size, :] = flip_ref[p]
        second_ref[0] = flip_ref[per:].reshape(chans, half).T

    outs = (
        jax.ShapeDtypeStruct((2, chans, half), F32),
        jax.ShapeDtypeStruct((2, half, chans), F32),
    )
    earlier = () if earlier is None else tuple(earlier)
    return pl.pallas_call(
        kernel,
        grid=(1,),
        in_specs=[SM, VM, VM] + [pl.BlockSpec(memory_space=pl.ANY)] * len(earlier),
        out_specs=(
            pl.BlockSpec((1, chans, half), lambda i: (b, 0, 0)),
            pl.BlockSpec((1, half, chans), lambda i: (b, 0, 0)),
        ),
        out_shape=outs,
        scratch_shapes=[pltpu.VMEM((pieces, size, half), F32)],
        input_output_aliases={3 + n: n for n in range(len(earlier))},
        cost_estimate=cost(1.5),
        compiler_params=pltpu.CompilerParams(vmem_limit_bytes=12 * 2**20),
        name="unpack",
    )(meta, mine, got, *earlier)


def lon_halo(block):
    count = lax.axis_size("lon")
    forward = [(i, (i + 1) % count) for i in range(count)]
    backward = [(target, source) for source, target in forward]
    size = block.shape[1]
    low = lax.ppermute(block[:, size - 12 :], "lon", forward)
    high = lax.ppermute(block[:, :12], "lon", backward)
    return low, high


def lat_halo(block, low, high):
    count = lax.axis_size("lat")
    index = lax.axis_index("lat")
    rows = block.shape[0]

    def strip(first):
        parts = [low, block, high]
        return jnp.concatenate(
            [lax.dynamic_slice_in_dim(x, first, 12, 0) for x in parts], axis=1
        )

    if count == 1:
        return [], []
    if count == 2:
        sent = strip((1 - index) * (rows - 12))
        got = lax.ppermute(sent, "lat", [(0, 1), (1, 0)])
        return [((index == 0).astype(jnp.int32), got)], [sent]
    down = [(i, i + 1) for i in range(count - 1)]
    up = [(target, source) for source, target in down]
    sent = [strip(rows - 12), strip(0)]
    above = lax.ppermute(sent[0], "lat", down)
    below = lax.ppermute(sent[1], "lat", up)
    return [(jnp.int32(0), above), (jnp.int32(1), below)], sent


def halos(block):
    low, high = lon_halo(block)
    return low, high, lat_halo(block, low, high)[0]


def convolve(me, block, halo, weights, base=None):
    low, high, gots = halo
    sums = conv_local(block, low, high, weights)
    if not gots:
        gots = [(jnp.int32(0), jnp.zeros((12, block.shape[1] + 24, block.shape[2]), BF))]
    for n, (below, got) in enumerate(gots):
        last = n == len(gots) - 1
        meta = jnp.stack([below, me])
        sums = conv_remote(meta, sums, got, weights, base if last else None, last)
    return sums


def swap(x):
    return lax.ppermute(x, "ch", [(0, 1), (1, 0)])


def flat(x):
    return x.reshape(-1, x.shape[-1])


def exchanges():
    lon = lax.axis_size("lon")
    lat = lax.axis_size("lat")
    along = [("lon", 2**n) for n in range(lon.bit_length() - 1)]
    across = [("lat", 2**n) for n in range(lat.bit_length() - 1)]
    return along[:1] + across + along[1:]


def partner(x, axis, dist):
    count = lax.axis_size(axis)
    return lax.ppermute(x, axis, [(i, i ^ dist) for i in range(count)])


def scatter_sum(part):
    for axis, dist in exchanges():
        half = part.shape[0] // 2
        part = part[:half] + partner(part[half:].astype(BF), axis, dist).astype(F32)
    return part.astype(BF)


def gather(part, extra=None):
    got = None
    for axis, dist in reversed(exchanges()):
        if got is not None:
            part = jnp.concatenate([part, got])
        rows = part.shape[0]
        if extra is None:
            got = partner(part, axis, dist)
        else:
            both = partner(jnp.concatenate([part, extra.astype(BF)]), axis, dist)
            got = both[:rows]
            extra = extra.astype(BF).astype(F32) + both[rows:].astype(F32)
        part, got, extra = yield part, got, extra


def advance(walk, state, steps=None):
    count = 0
    while steps is None or count < steps:
        try:
            state = walk.send(state)
        except StopIteration:
            break
        count += 1
    return state


def after(x, *first):
    return lax.optimization_barrier((x,) + first)[0]


def on_device(inputs, cotangent, kernels, gains, w_in, w_out):
    rows, breadth, own = inputs.shape
    scaling = 1.0 / math.sqrt(
        rows * lax.axis_size("lat") * breadth * lax.axis_size("lon")
    )
    me = lax.axis_index("ch")
    steps = exchanges()
    pieces = 2 ** len(steps)
    bits = 0
    for axis, dist in steps:
        bits = 2 * bits + (lax.axis_index(axis) // dist) % 2
    place = jnp.stack([me, me, bits])

    halo0 = halos(inputs)
    weights = (w_in, swap(w_in), w_out, swap(w_out), gains)
    taps = kernels.astype(F32)
    taps_back = taps[:, ::-1]

    def split(field):
        send = lax.dynamic_slice_in_dim(field, (1 - me) * (rows // 2), rows // 2, 0)
        return flat(field), swap(flat(send))

    def join(mine, send):
        theirs = swap(send)
        pair = jnp.where(
            me == 0, jnp.concatenate([mine, theirs]), jnp.concatenate([theirs, mine])
        )
        return pair.reshape(rows, breadth, own)

    def forward(b, block, halo):
        field, send = convolve(me, block, halo, taps[b])
        return flat(field), swap(flat(send))

    def scattered(keep, give):
        return scatter_sum(flat(keep) + swap(flat(give)).astype(F32))

    def kernel_sums(grad, block, halo):
        low, high, gots = halo
        meta = jnp.stack([below for below, _ in gots] + [me])
        return tap_sums(meta, grad, block, low, high, [got for _, got in gots])

    def spread_back(b, mine, send, block, halo, base):
        dconv = join(mine, send)
        low, high = lon_halo(dconv)
        gots, sent = lat_halo(dconv, low, high)
        dk = kernel_sums(after(dconv, low, high, *sent), block, halo)
        gots = [(below, after(got, dk)) for below, got in gots]
        field, send = convolve(me, dconv, (low, high, gots), taps_back[b], base)
        return field, send, dk

    conv0 = forward(0, inputs, halo0)
    grad2 = split(cotangent)
    mixed = mix_forward(0, place, *conv0, weights)
    current = (inputs.astype(F32) + join(*mixed).astype(F32)).astype(BF)
    halo1 = halos(current)
    conv1 = forward(1, current, halo1)

    mine, send, keep, give = mix_backward(1, place, *conv1, *grad2, weights, pieces, False)
    sums1 = scattered(keep, give)
    grad1, send, dk1 = spread_back(1, mine, send, current, halo1, cotangent)
    walk = gather(sums1)
    state = advance(walk, None, len(steps) - 2)
    other = swap(flat(send))
    if state is not None:
        other, *state = lax.optimization_barrier((other, state[0], state[1]))
        state = (*state, None)
    dpre, keep, give = mix_backward(
        0, place, *conv0, flat(grad1), other, weights, pieces, True
    )
    state = advance(walk, state, 1)
    dpre, *state = lax.optimization_barrier((dpre, state[0], state[1]))
    state = (*state, None)
    mine, send = mix_inputs(0, place, *conv0, dpre, weights)
    part1, got1, _ = advance(walk, state)
    sums0 = scattered(keep, give)
    grad0, _, dk0 = spread_back(0, mine, send, inputs, halo0, grad1)

    walk = gather(sums0, jnp.concatenate([dk0, dk1]))
    outs = unpack(1, place, part1, got1, scaling, pieces)
    part0, got0, dk = advance(walk, None)
    outs = unpack(0, place, part0, got0, scaling, pieces, outs)
    dk = dk.reshape(2, -1, own)[:, :49] * scaling
    return grad0, outs[0], outs[1], dk


def solution(mesh):
    return jax.shard_map(
        on_device,
        mesh=mesh,
        in_specs=(
            P(("grp", "lat"), "lon", "ch"),
            P(("grp", "lat"), "lon", "ch"),
            P(None, None, "ch"),
            P(),
            P(None, None, "ch"),
            P(None, "ch", None),
        ),
        out_specs=(
            P(("grp", "lat"), "lon", "ch"),
            P("grp", None, "ch"),
            P("grp", "ch", None),
            P("grp", None, "ch"),
        ),
        check_vma=False,
    )
```

```python
import math

import jax
import jax.numpy as jnp
from jax import lax
from jax.experimental import pallas as pl
from jax.experimental.pallas import tpu as pltpu
from jax.sharding import PartitionSpec as P

BF = jnp.bfloat16
F32 = jnp.float32


TILE = 32


def cost(us):
    return pl.CostEstimate(flops=int(us * 1e9), transcendentals=0, bytes_accessed=1 << 20)


def call(kernel, us, grant, **kwargs):
    return pl.pallas_call(
        kernel,
        cost_estimate=cost(us),
        compiler_params=pltpu.CompilerParams(vmem_limit_bytes=grant * 2**20),
        **kwargs,
    )


VM = pl.BlockSpec(memory_space=pltpu.VMEM)
SM = pl.BlockSpec(memory_space=pltpu.SMEM)


def spread(wide, shifted, rows, pieces):
    for first, value in pieces:
        wide[:, first : first + value.shape[1], :] = value[...].astype(F32)
    shifted[...] = wide[:, 4 : 4 + shifted.shape[1], :]


def window(wide, shifted, row, tile, col_tap, cols):
    if col_tap % 2:
        return wide[row, pl.ds(pl.multiple_of(tile * cols + 4 * col_tap + 4, 8), cols), :]
    return shifted[row, pl.ds(pl.multiple_of(tile * cols + 4 * col_tap, 8), cols), :]


def wide_shapes(rows, breadth):
    return [pltpu.VMEM((rows, breadth + 32, 128), F32), pltpu.VMEM((rows, breadth + 24, 128), F32)]


def conv_local(block, low, high, weights):
    rows, breadth, chans = block.shape
    groups = rows // 4

    def kernel(block_ref, low_ref, high_ref, w_ref, out_ref, wide, shifted):
        spread(wide, shifted, rows, ((16, block_ref), (4, low_ref), (16 + breadth, high_ref)))
        tiles = breadth // TILE

        def step(i, carry):
            cls, tile = i // tiles, i % tiles
            sums = [jnp.zeros((TILE // 8, 8, chans), F32) for _ in range(groups)]
            for q in range(7):
                taps = {}
                for r in range(groups):
                    v = window(wide, shifted, 4 * r + cls, tile, q, TILE).reshape(-1, 8, chans)
                    for k in range(groups):
                        p = r - k + 3
                        if 0 <= p <= 6:
                            if p not in taps:
                                taps[p] = w_ref[7 * p + q : 7 * p + q + 1, :]
                            sums[k] = sums[k] + taps[p] * v
            for k in range(groups):
                out_ref[4 * k + cls, pl.ds(pl.multiple_of(tile * TILE, 8), TILE), :] = sums[
                    k
                ].reshape(TILE, chans)
            return carry

        lax.fori_loop(0, 4 * tiles, step, 0)

    return call(
        kernel,
        2.5,
        8,
        in_specs=[VM] * 4,
        out_specs=VM,
        out_shape=jax.ShapeDtypeStruct(block.shape, F32),
        scratch_shapes=wide_shapes(rows, breadth),
        name="conv_local",
    )(block, low, high, weights)


def conv_remote(meta, sums_in, got, weights, base=None, last=True):
    rows, breadth, chans = sums_in.shape
    groups = rows // 4
    half = rows // 2

    def kernel(meta_ref, sums_ref, got_ref, w_ref, *rest):
        if base is not None:
            base_ref, rest = rest[0], rest[1:]
        if last:
            out_ref, send_ref, wide, shifted = rest
        else:
            out_ref, wide, shifted = rest
        below = meta_ref[0]
        spread(wide, shifted, 12, ((4, got_ref),))
        tiles = breadth // TILE

        def mirror(x, most):
            return x + below * (most - 2 * x)

        def step(i, carry):
            cls, tile = i // tiles, i % tiles
            cols = pl.ds(pl.multiple_of(tile * TILE, 8), TILE)
            at = [4 * mirror(k, groups - 1) + cls for k in range(groups)]
            sums = [sums_ref[at[k], cols, :].reshape(-1, 8, chans) for k in range(groups)]
            for q in range(7):
                taps = [w_ref[pl.ds(7 * mirror(p, 6) + q, 1), :] for p in range(3)]
                for r in range(3):
                    v = window(wide, shifted, 4 * mirror(r, 2) + cls, tile, q, TILE)
                    v = v.reshape(-1, 8, chans)
                    for k in range(min(groups, r + 1)):
                        sums[k] = sums[k] + taps[r - k] * v
            for k in range(groups):
                value = sums[k].reshape(TILE, chans)
                if base is not None:
                    value = value + base_ref[at[k], cols, :].astype(F32)
                out_ref[at[k], cols, :] = value.astype(out_ref.dtype)
            return carry

        lax.fori_loop(0, 4 * tiles, step, 0)
        if last:
            send_ref[...] = out_ref[pl.ds((1 - meta_ref[1]) * half, half)]

    field = jax.ShapeDtypeStruct((rows, breadth, chans), BF if last else F32)
    part = jax.ShapeDtypeStruct((half, breadth, chans), BF)
    args = (meta, sums_in, got, weights) + (() if base is None else (base,))
    return call(
        kernel,
        1.7,
        10,
        in_specs=[SM] + [VM] * (len(args) - 1),
        out_specs=(VM, VM) if last else VM,
        out_shape=(field, part) if last else field,
        scratch_shapes=wide_shapes(12, breadth),
        name="conv_remote",
    )(*args)


def tap_sums(meta, grad, block, low, high, gots):
    rows, breadth, chans = block.shape
    groups = rows // 4
    count = len(gots)

    def kernel(meta_ref, grad_ref, block_ref, low_ref, high_ref, *rest):
        got_refs, (packed_ref, out_ref, g_ref, wide, shifted, rwide, rshifted) = (
            rest[:count],
            rest[count:],
        )
        out_ref[48:] = jnp.zeros((16, chans), F32)
        g_ref[...] = grad_ref[...].astype(F32)
        spread(wide, shifted, rows, ((16, block_ref), (4, low_ref), (16 + breadth, high_ref)))
        tiles = breadth // 8

        def near(cols_taps):
            def step(i, sums):
                cls, tile = i // tiles, i % tiles
                sums = list(sums)
                cols = pl.ds(pl.multiple_of(tile * 8, 8), 8)
                g = [g_ref[4 * k + cls, cols, :] for k in range(groups)]
                for n, q in enumerate(cols_taps):
                    for r in range(groups):
                        v = window(wide, shifted, 4 * r + cls, tile, q, 8)
                        for k in range(groups):
                            p = r - k + 3
                            if 0 <= p <= 6:
                                sums[7 * n + p] = sums[7 * n + p] + g[k] * v
                return tuple(sums)

            zero = jnp.zeros((8, chans), F32)
            sums = lax.fori_loop(0, 4 * tiles, step, (zero,) * (7 * len(cols_taps)))
            for n, q in enumerate(cols_taps):
                for p in range(7):
                    out_ref[7 * p + q : 7 * p + q + 1, :] = jnp.sum(
                        sums[7 * n + p], axis=0, keepdims=True
                    )

        def far(index, cols_taps):
            below = meta_ref[index]

            def mirror(x, most):
                return x + below * (most - 2 * x)

            def step(i, sums):
                cls, tile = i // tiles, i % tiles
                sums = list(sums)
                cols = pl.ds(pl.multiple_of(tile * 8, 8), 8)
                near_k = range(min(3, groups))
                g = [g_ref[4 * mirror(k, groups - 1) + cls, cols, :] for k in near_k]
                for n, q in enumerate(cols_taps):
                    for r in range(3):
                        v = window(rwide, rshifted, 4 * mirror(r, 2) + cls, tile, q, 8)
                        for k in near_k:
                            if k <= r:
                                sums[3 * n + r - k] = sums[3 * n + r - k] + g[k] * v
                return tuple(sums)

            zero = jnp.zeros((8, chans), F32)
            sums = lax.fori_loop(0, 4 * tiles, step, (zero,) * (3 * len(cols_taps)))
            for n, q in enumerate(cols_taps):
                for p in range(3):
                    at = pl.ds(7 * mirror(p, 6) + q, 1)
                    out_ref[at, :] = out_ref[at, :] + jnp.sum(
                        sums[3 * n + p], axis=0, keepdims=True
                    )

        for cols_taps in ((0, 2, 4, 6), (1, 3, 5)):
            near(cols_taps)
        for index in range(count):
            spread(rwide, rshifted, 12, ((4, got_refs[index]),))
            far(index, tuple(range(7)))
        for lane in range(4):
            packed_ref[:, lane * chans : (lane + 1) * chans] = out_ref[pl.ds(lane, 16, stride=4), :]

    return call(
        kernel,
        6.8,
        14,
        in_specs=[SM] + [VM] * (4 + count),
        out_specs=VM,
        out_shape=jax.ShapeDtypeStruct((16, 4 * chans), F32),
        scratch_shapes=[pltpu.VMEM((64, chans), F32), pltpu.VMEM(block.shape, F32)]
        + wide_shapes(rows, breadth)
        + wide_shapes(12, breadth),
        name="tap_sums",
    )(meta, grad, block, low, high, *gots)


CUBIC = 0.044715
ROOT = math.sqrt(2.0 / math.pi)


def layer_norm(x):
    centred = x - jnp.mean(x, axis=-1, keepdims=True)
    inverse = lax.rsqrt(jnp.mean(centred * centred, axis=-1, keepdims=True) + 1e-06)
    return centred * inverse, inverse


def mxu(a, b):
    return jnp.dot(a, b, preferred_element_type=F32)


def cell_specs(cells, chans):
    mine = pl.BlockSpec((cells, chans), lambda i, meta: (meta[1], 0))
    theirs = pl.BlockSpec((cells, chans), lambda i, meta: (0, 0))
    return mine, theirs


def whole(shape):
    return pl.BlockSpec(shape, lambda i, meta: (0,) * len(shape))


def one_step(kernel, us, grant, in_specs, out_specs, out_shape, name, scratch=()):
    return pl.pallas_call(
        kernel,
        grid_spec=pltpu.PrefetchScalarGridSpec(
            num_scalar_prefetch=1,
            grid=(1,),
            in_specs=in_specs,
            out_specs=out_specs,
            scratch_shapes=list(scratch),
        ),
        out_shape=out_shape,
        cost_estimate=cost(us),
        compiler_params=pltpu.CompilerParams(vmem_limit_bytes=grant * 2**20),
        name=name,
    )


def natural(me, a, b):
    first = me == 0
    return jnp.concatenate([jnp.where(first, a, b), jnp.where(first, b, a)], axis=1)


def deal(me, x, own_ref, send_ref):
    chans = x.shape[1] // 2
    left, right = x[:, :chans], x[:, chans:]
    own_ref[...] = jnp.where(me == 0, left, right).astype(BF)
    send_ref[...] = jnp.where(me == 0, right, left).astype(BF)


def fold(a, b, left, right):
    return lax.dot_general(a, b, (((left,), (right,)), ((), ())), preferred_element_type=F32)


def weight_specs(b, weights):
    specs = [
        pl.BlockSpec((1,) + w.shape[1:], lambda i, meta: (b, 0, 0)) for w in weights[:4]
    ]
    return specs + [whole(weights[4].shape)]


CHUNK = 256


def chunks(weights):
    wi0, wi1, wo0, wo1 = weights
    count = wi0.shape[2] // CHUNK
    for n, (wi, wo) in enumerate(((wi0, wo0), (wi1, wo1))):
        for c in range(count):
            at = slice(c * CHUNK, (c + 1) * CHUNK)
            yield n, at, wi[0, :, at], wo[0, at, :]


def mix_forward(b, meta, field, other, weights):
    cells, chans = other.shape
    mine, theirs = cell_specs(cells, chans)

    def kernel(meta_ref, a_ref, b_ref, wi0, wi1, wo0, wo1, gain_ref, own_ref, send_ref):
        me = meta_ref[1]
        x = natural(me, a_ref[...].astype(F32), b_ref[...].astype(F32))
        y = (layer_norm(x)[0] * gain_ref[b : b + 1]).astype(BF)
        mixed = None
        for _, _, wi, wo in chunks((wi0, wi1, wo0, wo1)):
            pre = mxu(y, wi)
            tanh = jnp.tanh(pre * (ROOT + (ROOT * CUBIC) * (pre * pre)))
            hid = (pre * (0.5 + 0.5 * tanh)).astype(BF)
            part = mxu(hid, wo)
            mixed = part if mixed is None else mixed + part
        deal(me, mixed, own_ref, send_ref)

    return one_step(
        kernel,
        4,
        24,
        [mine, theirs] + weight_specs(b, weights),
        [theirs, theirs],
        [jax.ShapeDtypeStruct((cells, chans), BF)] * 2,
        "mix_forward",
    )(meta, field, other, *weights)


def hidden_back(y, g, wi, wo):
    pre = mxu(y, wi)
    square = pre * pre
    tanh = jnp.tanh(pre * (ROOT + (ROOT * CUBIC) * square))
    gate = 0.5 + 0.5 * tanh
    act = pre * gate
    slope = gate + (act - act * gate) * (2 * ROOT + (6 * ROOT * CUBIC) * square)
    return act.astype(BF), (fold(g, wo, 1, 1) * slope).astype(BF)


def norm_back(me, dy, gains, xhat, inverse, own_ref, send_ref):
    e = dy * gains
    centre = jnp.mean(e, axis=-1, keepdims=True)
    tilt = jnp.mean(e * xhat, axis=-1, keepdims=True)
    deal(me, (e - centre - xhat * tilt) * inverse, own_ref, send_ref)


def mix_backward(b, meta, field, other, gfield, gother, weights, pieces, late):
    cells, chans = other.shape
    half = weights[0].shape[2]
    size = 4 * chans // pieces
    mine, theirs = cell_specs(cells, chans)

    def kernel(meta_ref, a_ref, b_ref, ga_ref, gb_ref, wi0, wi1, wo0, wo1, gain_ref, *rest):
        *first, keep_ref, give_ref, acc_ref = rest
        me = meta_ref[1]
        gains = gain_ref[b : b + 1]
        x = natural(me, a_ref[...].astype(F32), b_ref[...].astype(F32))
        xhat, inverse = layer_norm(x)
        y = (xhat * gains).astype(BF)
        g = natural(me, ga_ref[...], gb_ref[...])
        dy = None
        for n, at, wi, wo in chunks((wi0, wi1, wo0, wo1)):
            hid, dpre = hidden_back(y, g, wi, wo)
            acc_ref[n, : 2 * chans, at] = fold(y, dpre, 0, 0)
            acc_ref[n, 2 * chans :, at] = fold(g, hid, 0, 0)
            if late:
                first[0][n, :, at] = dpre
            else:
                part = fold(dpre, wi, 1, 1)
                dy = part if dy is None else dy + part
        if not late:
            norm_back(me, dy, gains, xhat, inverse, *first)
        bits = meta_ref[2]
        for p in range(pieces):
            rows = slice(p * size, (p + 1) * size)
            keep_ref[p ^ bits] = acc_ref[0, rows]
            give_ref[p ^ bits] = acc_ref[1, rows].astype(BF)

    grads = whole((pieces, size, half))
    cell = jax.ShapeDtypeStruct((cells, chans), BF)
    return one_step(
        kernel,
        7 if late else 9,
        36,
        [mine, theirs, mine, theirs] + weight_specs(b, weights),
        ([whole((2, cells, half))] if late else [theirs, theirs]) + [grads, grads],
        ([jax.ShapeDtypeStruct((2, cells, half), BF)] if late else [cell, cell])
        + [
            jax.ShapeDtypeStruct((pieces, size, half), F32),
            jax.ShapeDtypeStruct((pieces, size, half), BF),
        ],
        "mix_weights" if late else "mix_backward",
        [pltpu.VMEM((2, 4 * chans, half), F32)],
    )(meta, field, other, gfield, gother, *weights)


def mix_inputs(b, meta, field, other, dpre, weights):
    cells, chans = other.shape
    mine, theirs = cell_specs(cells, chans)

    def kernel(meta_ref, a_ref, b_ref, dpre_ref, wi0, wi1, gain_ref, own_ref, send_ref):
        me = meta_ref[1]
        x = natural(me, a_ref[...].astype(F32), b_ref[...].astype(F32))
        xhat, inverse = layer_norm(x)
        dy = fold(dpre_ref[0], wi0[0], 1, 1) + fold(dpre_ref[1], wi1[0], 1, 1)
        norm_back(me, dy, gain_ref[b : b + 1], xhat, inverse, own_ref, send_ref)

    specs = weight_specs(b, weights)
    return one_step(
        kernel,
        3,
        24,
        [mine, theirs, whole(dpre.shape), specs[0], specs[1], specs[4]],
        [theirs, theirs],
        [jax.ShapeDtypeStruct((cells, chans), BF)] * 2,
        "mix_inputs",
    )(meta, field, other, dpre, weights[0], weights[1], weights[4])


def unpack(b, meta, mine, got, scaling, pieces, earlier=None, extra=None):
    rows, half = mine.shape
    size = 2 * rows // pieces
    chans = pieces * size // 2
    per = pieces // 2

    def kernel(meta_ref, mine_ref, got_ref, *rest):
        if extra is None:
            first_ref, second_ref, flip_ref = rest[-3:]
        else:
            extra_ref, taps_ref = rest[0], rest[-2]
            first_ref, second_ref, flip_ref = rest[-4], rest[-3], rest[-1]
            total = (extra_ref[...].astype(F32) + got_ref[rows:, :].astype(F32)) * scaling
            lanes = half // 4
            for block in range(2):
                for lane in range(4):
                    count = 13 if lane == 0 else 12
                    taps_ref[block, pl.ds(lane, count, stride=4), :] = total[
                        16 * block : 16 * block + count, lane * lanes : (lane + 1) * lanes
                    ]
        bits = meta_ref[2]
        for r in range(pieces):
            source = mine_ref if r < per else got_ref
            at = (r % per) * size
            flip_ref[r ^ bits] = source[at : at + size, :].astype(F32) * scaling
        for p in range(per):
            first_ref[0, p * size : (p + 1) * size, :] = flip_ref[p]
        second_ref[0] = flip_ref[per:].reshape(chans, half).T

    outs = [
        jax.ShapeDtypeStruct((2, chans, half), F32),
        jax.ShapeDtypeStruct((2, half, chans), F32),
    ]
    out_specs = [
        pl.BlockSpec((1, chans, half), lambda i: (b, 0, 0)),
        pl.BlockSpec((1, half, chans), lambda i: (b, 0, 0)),
    ]
    args = [meta, mine, got]
    if extra is not None:
        args.append(extra)
        outs.append(jax.ShapeDtypeStruct((2, 49, half // 4), F32))
        out_specs.append(VM)
    specs = [SM] + [VM] * (len(args) - 1)
    count = len(args)
    earlier = () if earlier is None else tuple(earlier)
    return pl.pallas_call(
        kernel,
        grid=(1,),
        in_specs=specs + [pl.BlockSpec(memory_space=pl.ANY)] * len(earlier),
        out_specs=out_specs,
        out_shape=outs,
        scratch_shapes=[pltpu.VMEM((pieces, size, half), F32)],
        input_output_aliases={count + n: n for n in range(len(earlier))},
        cost_estimate=cost(1.5),
        compiler_params=pltpu.CompilerParams(vmem_limit_bytes=12 * 2**20),
        name="unpack",
    )(*args, *earlier)


def lon_halo(block):
    count = lax.axis_size("lon")
    forward = [(i, (i + 1) % count) for i in range(count)]
    backward = [(target, source) for source, target in forward]
    size = block.shape[1]
    low = lax.ppermute(block[:, size - 12 :], "lon", forward)
    high = lax.ppermute(block[:, :12], "lon", backward)
    return low, high


def lat_halo(block, low, high):
    count = lax.axis_size("lat")
    index = lax.axis_index("lat")
    rows = block.shape[0]

    def strip(first):
        parts = [low, block, high]
        return jnp.concatenate(
            [lax.dynamic_slice_in_dim(x, first, 12, 0) for x in parts], axis=1
        )

    if count == 1:
        return [], []
    if count == 2:
        sent = strip((1 - index) * (rows - 12))
        got = lax.ppermute(sent, "lat", [(0, 1), (1, 0)])
        return [((index == 0).astype(jnp.int32), got)], [sent]
    down = [(i, i + 1) for i in range(count - 1)]
    up = [(target, source) for source, target in down]
    sent = [strip(rows - 12), strip(0)]
    above = lax.ppermute(sent[0], "lat", down)
    below = lax.ppermute(sent[1], "lat", up)
    return [(jnp.int32(0), above), (jnp.int32(1), below)], sent


def halos(block):
    low, high = lon_halo(block)
    return low, high, lat_halo(block, low, high)[0]


def convolve(me, block, halo, weights, base=None):
    low, high, gots = halo
    sums = conv_local(block, low, high, weights)
    if not gots:
        gots = [(jnp.int32(0), jnp.zeros((12, block.shape[1] + 24, block.shape[2]), BF))]
    for n, (below, got) in enumerate(gots):
        last = n == len(gots) - 1
        meta = jnp.stack([below, me])
        sums = conv_remote(meta, sums, got, weights, base if last else None, last)
    return sums


def swap(x):
    return lax.ppermute(x, "ch", [(0, 1), (1, 0)])


def flat(x):
    return x.reshape(-1, x.shape[-1])


def exchanges(b):
    lon = lax.axis_size("lon")
    lat = lax.axis_size("lat")
    along = [("lon", 2**n) for n in range(lon.bit_length() - 1)]
    across = [("lat", 2**n) for n in range(lat.bit_length() - 1)]
    return across + along if b == 0 else along[:1] + across + along[1:]


def partner(x, axis, dist):
    count = lax.axis_size(axis)
    return lax.ppermute(x, axis, [(i, i ^ dist) for i in range(count)])


def after(x, *first):
    return lax.optimization_barrier((x,) + first)[0]


def halve(b, part, *earlier):
    axis, dist = exchanges(b)[0]
    half = part.shape[0] // 2
    send = after(part[half:].astype(BF), *earlier)
    return part[:half], send, partner(send, axis, dist)


def scatter_sum(b, part, got):
    part = part + got.astype(F32)
    for axis, dist in exchanges(b)[1:]:
        half = part.shape[0] // 2
        part = part[:half] + partner(part[half:].astype(BF), axis, dist).astype(F32)
    return part.astype(BF)


def gather(steps, part, got=None):
    for axis, dist in steps:
        if got is not None:
            part = jnp.concatenate([part, got])
        got = partner(part, axis, dist)
    return part, got


def gather_with(steps, part, extra):
    both = None
    for axis, dist in steps:
        extra = extra.astype(BF)
        if both is not None:
            rows = part.shape[0]
            part = jnp.concatenate([part, both[:rows]])
            extra = (extra.astype(F32) + both[rows:].astype(F32)).astype(BF)
        both = partner(jnp.concatenate([part, extra]), axis, dist)
    return part, both, extra


def on_device(inputs, cotangent, kernels, gains, w_in, w_out):
    rows, breadth, own = inputs.shape
    scaling = 1.0 / math.sqrt(
        rows * lax.axis_size("lat") * breadth * lax.axis_size("lon")
    )
    me = lax.axis_index("ch")
    pieces = 2 ** len(exchanges(0))
    place = []
    for b in range(2):
        bits = 0
        for axis, dist in exchanges(b):
            bits = 2 * bits + (lax.axis_index(axis) // dist) % 2
        place.append(jnp.stack([me, me, bits]))

    halo0 = halos(inputs)
    weights = (w_in, swap(w_in), w_out, swap(w_out), gains)
    taps = kernels.astype(F32)
    taps_back = taps[:, ::-1]

    def split(field):
        send = lax.dynamic_slice_in_dim(field, (1 - me) * (rows // 2), rows // 2, 0)
        return flat(field), swap(flat(send))

    def join(mine, send):
        theirs = swap(send)
        pair = jnp.where(
            me == 0, jnp.concatenate([mine, theirs]), jnp.concatenate([theirs, mine])
        )
        return pair.reshape(rows, breadth, own)

    def forward(b, block, halo):
        field, send = convolve(me, block, halo, taps[b])
        return flat(field), swap(flat(send))

    def halved(b, keep, give, *earlier):
        return halve(b, flat(keep) + swap(flat(give)).astype(F32), *earlier)

    def kernel_sums(grad, block, halo):
        low, high, gots = halo
        meta = jnp.stack([below for below, _ in gots] + [me])
        return tap_sums(meta, grad, block, low, high, [got for _, got in gots])

    def spread_back(b, mine, send, first, block, halo, base):
        dconv = join(mine, send)
        low, high = lon_halo(dconv)
        gots, sent = lat_halo(dconv, low, high)
        ahead = (low, high, *sent) if b else (first,)
        dk = kernel_sums(after(dconv, *ahead), block, halo)
        gots = [(below, after(got, dk)) for below, got in gots]
        field, send = convolve(me, dconv, (low, high, gots), taps_back[b], base)
        return field, send, dk, sent

    conv0 = forward(0, inputs, halo0)
    grad2 = split(cotangent)
    mixed = mix_forward(0, place[0], *conv0, weights)
    current = (inputs.astype(F32) + join(*mixed).astype(F32)).astype(BF)
    halo1 = halos(current)
    conv1 = forward(1, current, halo1)

    mine, send, keep, give = mix_backward(1, place[1], *conv1, *grad2, weights, pieces, False)
    kept, first, came = halved(1, keep, give)
    sums1 = scatter_sum(1, kept, came)
    grad1, send, dk1, _ = spread_back(1, mine, send, first, current, halo1, cotangent)
    other = after(swap(flat(send)), sums1)
    dpre, keep, give = mix_backward(
        0, place[0], *conv0, flat(grad1), other, weights, pieces, True
    )
    steps = exchanges(1)[::-1]
    part1, got1 = gather(steps[:1], sums1)
    dpre, part1, got1 = lax.optimization_barrier((dpre, part1, got1))
    mine, send = mix_inputs(0, place[0], *conv0, dpre, weights)
    part1, got1 = gather(steps[1:-1], part1, got1)
    kept, first, came = halved(0, keep, give, got1)
    part1, got1, _ = lax.optimization_barrier((part1, got1, first))
    part1, got1 = gather(steps[-1:], part1, got1)
    grad0, _, dk0, sent = spread_back(0, mine, send, first, inputs, halo0, grad1)
    sums0 = scatter_sum(0, kept, after(came, dk0, got1, *sent))

    outs = unpack(1, place[1], part1, got1, scaling, pieces)
    part0, got0, dk = gather_with(exchanges(0)[::-1], sums0, jnp.concatenate([dk0, dk1]))
    outs = unpack(0, place[0], part0, got0, scaling, pieces, outs, dk)
    return (grad0, *outs)


def solution(mesh):
    return jax.shard_map(
        on_device,
        mesh=mesh,
        in_specs=(
            P(("grp", "lat"), "lon", "ch"),
            P(("grp", "lat"), "lon", "ch"),
            P(None, None, "ch"),
            P(),
            P(None, None, "ch"),
            P(None, "ch", None),
        ),
        out_specs=(
            P(("grp", "lat"), "lon", "ch"),
            P("grp", None, "ch"),
            P("grp", "ch", None),
            P("grp", None, "ch"),
        ),
        check_vma=False,
    )
```
